768 devices in a mesh: ta: 128 (over z_lo, y, x), gz: 6 (over z_hi, core).
Axes of the slice: x: 4, y: 8, z: 12 (z_hi: 3, z_lo: 4; z = z_hi * 4 + z_lo), core: 2. Of those that a mesh axis runs over, the one named last changes fastest.
Arguments:
- links: float32 [4, 2, 3, 3, 128, 12, 128], P(None, None, None, None, 'ta', 'gz'), may hold values from -1 to 1, as said below
Outputs:
- flowed: float32 [4, 2, 3, 3, 128, 12, 128], P(None, None, None, None, 'ta', 'gz')
- loops: float32 [2, 3, 3, 128, 12, 128], P(None, None, None, 'ta', 'gz')
The draws below stay inside these ranges and needn't reach their ends.
Inputs may be any that keep to these rules, and one draw needn't show every extreme that they name: `links`: every link is a special unitary 3x3 matrix, given by its real and imaginary parts.
All inputs are finite; a program needn't handle non-finite values.
Results may differ from the reference program's by a relative error of at most 0.0001.
Values sent between devices are 32-bit elements; how exact they have to be, the bound alone decides.
A program may use at most 32 MiB of HBM per device.

```python
import jax
import jax.numpy as jnp

LX = 8
LY = 16
NT = 128
NZ = 12


def real_product_drawn(left, right):
    return jnp.sum(left[:, :, None] * right[None, :, :], axis=1)


def product_drawn(left, right):
    real_part = real_product_drawn(left[0], right[0]) - real_product_drawn(left[1], right[1])
    imag_part = real_product_drawn(left[0], right[1]) + real_product_drawn(left[1], right[0])
    return jnp.stack([real_part, imag_part])


def subgroup(key, first, second, base, tail):
    normals = jax.random.normal(key, (4,) + tail, jnp.float32)
    head = base + jnp.abs(normals[0])
    rest = normals[1:]
    length = jnp.sqrt(head * head + jnp.sum(rest * rest, axis=0))
    quat_zero = head / length
    quat_one = rest[0] / length
    quat_two = rest[1] / length
    quat_three = rest[2] / length
    zeros = jnp.zeros(tail, jnp.float32)
    ones = jnp.ones(tail, jnp.float32)
    real_rows = [[ones, zeros, zeros], [zeros, ones, zeros], [zeros, zeros, ones]]
    imag_rows = [[zeros, zeros, zeros], [zeros, zeros, zeros], [zeros, zeros, zeros]]
    real_rows[first][first] = quat_zero
    imag_rows[first][first] = quat_three
    real_rows[first][second] = quat_two
    imag_rows[first][second] = quat_one
    real_rows[second][first] = -quat_two
    imag_rows[second][first] = quat_one
    real_rows[second][second] = quat_zero
    imag_rows[second][second] = -quat_three
    real_part = jnp.stack([jnp.stack(row) for row in real_rows])
    imag_part = jnp.stack([jnp.stack(row) for row in imag_rows])
    return jnp.stack([real_part, imag_part])


def draw_links(key, part):
    base = 0.5
    tail = (4, NT, NZ, LX * LY)
    first = subgroup(jax.random.fold_in(key, 11), 0, 1, base, tail)
    second = subgroup(jax.random.fold_in(key, 12), 1, 2, base, tail)
    third = subgroup(jax.random.fold_in(key, 13), 0, 2, base, tail)
    matrix = product_drawn(product_drawn(first, second), third)
    return jnp.transpose(matrix, (3, 0, 1, 2, 4, 5, 6)).astype(jnp.float32)


def setup_inputs(seed: int = 0) -> dict:
    seeds = jax.random.split(jax.random.key(seed), 2)
    links = draw_links(jax.random.fold_in(seeds[1], 71), 0)
    return dict(links=links)


def real_product(left, right):
    return jnp.sum(left[:, :, None] * right[None, :, :], axis=1)


def product(left, right):
    real_part = real_product(left[0], right[0]) - real_product(left[1], right[1])
    imag_part = real_product(left[0], right[1]) + real_product(left[1], right[0])
    return jnp.stack([real_part, imag_part])


def adjoint(matrix):
    return jnp.stack([jnp.swapaxes(matrix[0], 0, 1), -jnp.swapaxes(matrix[1], 0, 1)])


def identity_like(matrix):
    tail = matrix.shape[3:]
    eye_part = jnp.broadcast_to(jnp.eye(3, dtype=jnp.float32).reshape((3, 3) + (1,) * len(tail)), (3, 3) + tail)
    return jnp.stack([eye_part, jnp.zeros((3, 3) + tail, jnp.float32)])


def shifted(padded, direction, offset):
    field = padded[direction]
    steps = field.shape[-3] - 2
    depth = field.shape[-2] - 2
    core = field[..., 1 + offset[0]:1 + offset[0] + steps, 1 + offset[1]:1 + offset[1] + depth, :]
    if offset[2] != 0 or offset[3] != 0:
        grid = core.reshape(core.shape[:-1] + (LX, LY))
        grid = jnp.roll(grid, (-offset[2], -offset[3]), axis=(-2, -1))
        core = grid.reshape(core.shape)
    return core


def unit_step(direction):
    table = ((1, 0, 0, 0), (0, 0, 1, 0), (0, 0, 0, 1), (0, 1, 0, 0))
    return table[direction]


def traceless_part(omega):
    real_part = 0.5 * (omega[0] - jnp.swapaxes(omega[0], 0, 1))
    imag_part = 0.5 * (omega[1] + jnp.swapaxes(omega[1], 0, 1))
    trace_imag = (imag_part[0, 0] + imag_part[1, 1] + imag_part[2, 2]) / 3.0
    eye_part = jnp.eye(3, dtype=jnp.float32).reshape((3, 3) + (1,) * trace_imag.ndim)
    imag_part = imag_part - eye_part * trace_imag[None, None]
    return jnp.stack([real_part, imag_part])


def flow_links(padded):
    zero = (0, 0, 0, 0)
    results = []
    for direction in range(4):
        link = shifted(padded, direction, zero)
        step_main = unit_step(direction)
        total = jnp.zeros_like(link)
        for other in range(4):
            if other == direction:
                continue
            step_other = unit_step(other)
            minus_other = tuple(-value for value in step_other)
            cross = tuple(a - b for a, b in zip(step_main, step_other))
            upper = product(product(shifted(padded, other, step_main), adjoint(shifted(padded, direction, step_other))), adjoint(shifted(padded, other, zero)))
            lower = product(product(adjoint(shifted(padded, other, cross)), adjoint(shifted(padded, direction, minus_other))), shifted(padded, other, minus_other))
            total = total + upper + lower
        omega = product(link, total)
        generator = -0.25 * traceless_part(omega)
        unity = identity_like(link)
        series = unity
        for order in range(6, 0, -1):
            series = unity + product(generator, series) / float(order)
        results.append(product(series, link))
    return jnp.stack(results)


def local_chain(lines):
    count = lines.shape[3]
    slices = [lines[:, :, :, index] for index in range(count)]
    unity = identity_like(slices[0])
    prefixes = [unity]
    for index in range(count):
        prefixes.append(product(prefixes[-1], slices[index]))
    suffixes = [unity] * count
    suffix = unity
    for index in range(count - 1, -1, -1):
        suffix = product(slices[index], suffix)
        suffixes[index] = suffix
    return prefixes[count], prefixes, suffixes


def reference(links):
    widths = ((0, 0),) * 4 + ((1, 1), (1, 1), (0, 0))
    padded = jnp.pad(links, widths, mode="wrap")
    flowed = flow_links(padded)
    total, prefixes, suffixes = local_chain(flowed[0])
    count = flowed.shape[4]
    loops = jnp.stack([product(suffixes[index], prefixes[index]) for index in range(count)], axis=3)
    return flowed, loops
```

```python
import jax
import jax.numpy as jnp
from jax import lax
from jax.experimental import pallas as pl
from jax.experimental.pallas import tpu as pltpu
from jax.sharding import PartitionSpec as P

LX = 8
LY = 16
LANES = LX * LY
MESH = pl.DeviceIdType.MESH


def factors(count):
    first = 4 if count % 4 == 0 and count > 8 else 2
    rest = count // first
    third = 4 if rest % 4 == 0 and rest > 4 else 2
    return first, rest // third, third


def greet(peers):
    barrier = pltpu.get_barrier_semaphore()
    for peer in peers:
        pl.semaphore_signal(barrier, inc=1, device_id=peer, device_id_type=MESH)
    pl.semaphore_wait(barrier, len(peers))


def halo_kernel(count_t, count_z, u, tp, tm, zp, zm, cz, ct, send, recv):
    t = lax.axis_index("ta")
    z = lax.axis_index("gz")
    t_next, t_prev = lax.rem(t + 1, count_t), lax.rem(t + count_t - 1, count_t)
    z_next, z_prev = lax.rem(z + 1, count_z), lax.rem(z + count_z - 1, count_z)
    plan = [
        (u.at[pl.ds(3, 1)], cz, (t_prev, z_next)),
        (u.at[pl.ds(0, 1)], ct, (t_next, z_prev)),
        (u, zm, (t, z_next)),
        (u.at[pl.ds(0, 3)], zp, (t, z_prev)),
        (u, tm, (t_next, z)),
        (u.at[pl.ds(1, 3)], tp, (t_prev, z)),
    ]
    greet([peer for _, _, peer in plan])
    copies = [
        pltpu.make_async_remote_copy(
            src_ref=source,
            dst_ref=target,
            send_sem=send.at[index],
            recv_sem=recv.at[index],
            device_id=peer,
            device_id_type=MESH,
        )
        for index, (source, target, peer) in enumerate(plan)
    ]
    for copy in copies:
        copy.start()
    for copy in copies:
        copy.wait()


def halos(links, count_t, count_z):
    tail = links.shape[1:]
    shapes = [(n,) + tail for n in (3, 4, 3, 4, 1, 1)]
    return pl.pallas_call(
        lambda *refs: halo_kernel(count_t, count_z, *refs),
        out_shape=[jax.ShapeDtypeStruct(shape, jnp.float32) for shape in shapes],
        in_specs=[pl.BlockSpec(memory_space=pl.ANY)],
        out_specs=[pl.BlockSpec(memory_space=pl.ANY)] * 6,
        scratch_shapes=[pltpu.SemaphoreType.DMA((6,)), pltpu.SemaphoreType.DMA((6,))],
        compiler_params=pltpu.CompilerParams(collective_id=0, has_side_effects=True),
        name="halo_exchange",
    )(links)


def entry(matrix, row, col, adjoint):
    if adjoint:
        return matrix[col * 3 + row], matrix[9 + col * 3 + row], -1
    return matrix[row * 3 + col], matrix[9 + row * 3 + col], 1


def tile_product(left, right, left_adjoint=False, right_adjoint=False):
    real, imag = [], []
    for row in range(3):
        for col in range(3):
            re = im = None
            for mid in range(3):
                a, b, s = entry(left, row, mid, left_adjoint)
                c, d, r = entry(right, mid, col, right_adjoint)
                ac, bd, ad, bc = a * c, b * d, a * d, b * c
                re_term = ac - bd if s * r > 0 else ac + bd
                re = re_term if re is None else re + re_term
                if im is None:
                    if r > 0:
                        im = ad + bc if s > 0 else ad - bc
                    else:
                        im = bc - ad if s > 0 else -(ad + bc)
                else:
                    im = im + ad if r > 0 else im - ad
                    im = im + bc if s > 0 else im - bc
            real.append(re)
            imag.append(im)
    return real + imag


def flow_kernel(u, tp, tm, zp, zm, cz, ct, flowed, line, pk, fields):
    for i in range(18):
        for mu in range(4):
            rows = slice(2 * mu, 2 * mu + 2)
            pk[0, i, rows, :] = u[mu, i]
            pk[2, i, rows, :] = tm[mu, i]
            pk[4, i, 2 * mu : 2 * mu + 1, :] = zm[mu, i, 1:2]
            pk[4, i, 2 * mu + 1 : 2 * mu + 2, :] = u[mu, i, 0:1]
            if mu > 0:
                pk[1, i, rows, :] = tp[mu - 1, i]
            if mu < 3:
                pk[3, i, 2 * mu : 2 * mu + 1, :] = u[mu, i, 1:2]
                pk[3, i, 2 * mu + 1 : 2 * mu + 2, :] = zp[mu, i, 0:1]
        pk[5, i, 0:1, :] = tm[0, i, 1:2]
        pk[5, i, 1:2, :] = ct[0, i, 0:1]
        pk[5, i, 6:7, :] = cz[0, i, 1:2]
        pk[5, i, 7:8, :] = tp[2, i, 0:1]
    group = lax.broadcasted_iota(jnp.int32, (8, LANES), 0) // 2
    y = lax.broadcasted_iota(jnp.int32, (8, LANES), 1) % LY

    def pick(tiles):
        rest = jnp.where(group == 2, tiles[2], tiles[3])
        return jnp.where(group == 0, tiles[0], jnp.where(group == 1, tiles[1], rest))

    def x_plus(tile):
        return pltpu.roll(tile, LANES - LY, 1)

    def x_minus(tile):
        return pltpu.roll(tile, LY, 1)

    def y_plus(tile):
        return jnp.where(
            y == LY - 1, pltpu.roll(tile, LY - 1, 1), pltpu.roll(tile, LANES - 1, 1)
        )

    def y_minus(tile):
        return jnp.where(
            y == 0, pltpu.roll(tile, LANES - LY + 1, 1), pltpu.roll(tile, 1, 1)
        )

    def lowered(tile, k):
        return pltpu.roll(tile, 8 - 2 * k, 0)

    for i in range(18):
        here, t_up, t_down, z_up, z_down, corner = (pk[f, i] for f in range(6))
        up = [t_up, x_plus(here), y_plus(here), z_up]
        down = [t_down, x_minus(here), y_minus(here), z_down]
        base = pick(down)
        t_side = [None, corner, y_plus(t_down), x_plus(t_down)]
        z_side = [None, y_plus(z_down), x_plus(z_down), corner]
        for k in range(1, 4):
            ahead = pick([up[(nu - k) % 4] for nu in range(4)])
            behind = pick([down[(nu - k) % 4] for nu in range(4)])
            cross = pick([t_side[k], x_minus(ahead), y_minus(ahead), z_side[k]])
            fields[0, k - 1, i] = lowered(ahead, k)
            fields[1, 3 - k, i] = ahead
            fields[2, k - 1, i] = lowered(here, k)
            fields[3, k - 1, i] = lowered(cross, k)
            fields[4, 3 - k, i] = behind
            fields[5, k - 1, i] = lowered(base, k)

    def load(field, k):
        return [fields[field, k, i] for i in range(18)]

    total = None
    for k in range(3):
        upper = tile_product(load(0, k), load(1, k), False, True)
        upper = tile_product(upper, load(2, k), False, True)
        lower = tile_product(load(3, k), load(4, k), True, True)
        lower = tile_product(lower, load(5, k))
        both = [a + b for a, b in zip(upper, lower)]
        total = both if total is None else [a + b for a, b in zip(total, both)]
    link = [pk[0, i] for i in range(18)]
    omega = tile_product(link, total)
    trace = (omega[9] + omega[13] + omega[17]) * (1.0 / 3.0)
    generator = [None] * 18
    for row in range(3):
        for col in range(3):
            a, b = row * 3 + col, col * 3 + row
            generator[a] = -0.125 * (omega[a] - omega[b])
            part = 0.5 * (omega[9 + a] + omega[9 + b])
            if row == col:
                part = part - trace
            generator[9 + a] = -0.25 * part

    def plus_unity(matrix):
        return [v + 1.0 if i in (0, 4, 8) else v for i, v in enumerate(matrix)]

    series = plus_unity([v * (1.0 / 6.0) for v in generator])
    for order in range(5, 0, -1):
        series = tile_product(generator, series)
        series = plus_unity([v * (1.0 / order) for v in series])
    result = tile_product(series, link)
    for i in range(18):
        for mu in range(4):
            flowed[mu, i] = result[i][2 * mu : 2 * mu + 2]
        line[i] = result[i][0:2]


def flow(links, around):
    vmem = pl.BlockSpec(memory_space=pltpu.VMEM)
    return pl.pallas_call(
        flow_kernel,
        out_shape=[
            jax.ShapeDtypeStruct(links.shape, jnp.float32),
            jax.ShapeDtypeStruct(links.shape[1:], jnp.float32),
        ],
        in_specs=[vmem] * 7,
        out_specs=[vmem] * 2,
        scratch_shapes=[
            pltpu.VMEM((6, 18, 8, LANES), jnp.float32),
            pltpu.VMEM((6, 3, 18, 8, LANES), jnp.float32),
        ],
        name="flow_links",
    )(links, *around)


def product(left, right):
    re = im = None
    for mid in range(3):
        a, b = left[0][:, mid : mid + 1], left[1][:, mid : mid + 1]
        c, d = right[0][mid : mid + 1], right[1][mid : mid + 1]
        re_term, im_term = a * c - b * d, a * d + b * c
        re = re_term if re is None else re + re_term
        im = im_term if im is None else im + im_term
    return re, im


def loops_kernel(count, line, out, slots1, slots2, slots3, row_total, plane_total, send, recv):
    sizes = factors(count)
    t = lax.axis_index("ta")
    z = lax.axis_index("gz")
    strides = (1, sizes[0], sizes[0] * sizes[1])
    digits = [lax.rem(t // stride, size) for stride, size in zip(strides, sizes)]
    slots = (slots1, slots2, slots3)

    def peer(stage, offset):
        size, stride, digit = sizes[stage], strides[stage], digits[stage]
        moved = lax.rem(digit + size - offset, size)
        return (t + (moved - digit) * stride, z)

    greet([peer(s, d) for s in range(3) for d in range(1, sizes[s])])
    shape = (3, 3) + line.shape[-2:]
    diagonal = [
        [jnp.full(shape[2:], 1.0 if a == b else 0.0, jnp.float32) for b in range(3)]
        for a in range(3)
    ]
    unity = jnp.stack([jnp.stack(row) for row in diagonal])
    nought = jnp.zeros(shape, jnp.float32)
    start = [0, sizes[0] - 1, sizes[0] + sizes[1] - 2]

    def share(stage, source):
        copies = []
        for offset in range(1, sizes[stage]):
            index = start[stage] + offset - 1
            copies.append(
                pltpu.make_async_remote_copy(
                    src_ref=source,
                    dst_ref=slots[stage].at[offset - 1],
                    send_sem=send.at[index],
                    recv_sem=recv.at[index],
                    device_id=peer(stage, offset),
                    device_id_type=MESH,
                )
            )
        for copy in copies:
            copy.start()
        return copies

    def ordered(stage, copies):
        after = before = None
        for offset in range(1, sizes[stage]):
            copies[offset - 1].wait_recv()
            re, im = slots[stage][offset - 1, 0], slots[stage][offset - 1, 1]
            inside = digits[stage] + offset < sizes[stage]
            high = (jnp.where(inside, re, unity), jnp.where(inside, im, nought))
            low = (jnp.where(inside, unity, re), jnp.where(inside, nought, im))
            after = high if after is None else product(after, high)
            before = low if before is None else product(before, low)
        return after, before

    copies1 = share(0, line)
    row_after, row_before = ordered(0, copies1)
    row_after = product((line[0], line[1]), row_after)
    row = product(row_before, row_after)
    row_total[0], row_total[1] = row
    copies2 = share(1, row_total)
    plane_after, plane_before = ordered(1, copies2)
    plane = product(plane_before, product(row, plane_after))
    plane_total[0], plane_total[1] = plane
    copies3 = share(2, plane_total)
    left = product(row_after, plane_after)
    right = product(plane_before, row_before)
    for offset in range(1, sizes[2]):
        copies3[offset - 1].wait_recv()
        left = product(left, (slots3[offset - 1, 0], slots3[offset - 1, 1]))
    result = product(left, right)
    out[0], out[1] = result
    for copy in copies1 + copies2 + copies3:
        copy.wait_send()


def loops_of(line, count):
    sizes = factors(count)
    vmem = pl.BlockSpec(memory_space=pltpu.VMEM)
    messages = sum(sizes) - 3
    return pl.pallas_call(
        lambda *refs: loops_kernel(count, *refs),
        out_shape=jax.ShapeDtypeStruct(line.shape, jnp.float32),
        in_specs=[vmem],
        out_specs=vmem,
        scratch_shapes=[
            pltpu.VMEM((sizes[0] - 1,) + line.shape, jnp.float32),
            pltpu.VMEM((sizes[1] - 1,) + line.shape, jnp.float32),
            pltpu.VMEM((sizes[2] - 1,) + line.shape, jnp.float32),
            pltpu.VMEM(line.shape, jnp.float32),
            pltpu.VMEM(line.shape, jnp.float32),
            pltpu.SemaphoreType.DMA((messages,)),
            pltpu.SemaphoreType.DMA((messages,)),
        ],
        compiler_params=pltpu.CompilerParams(collective_id=1, has_side_effects=True),
        name="temporal_loops",
    )(line)


def local(links):
    count_t, count_z = lax.axis_size("ta"), lax.axis_size("gz")
    packed = links.reshape(4, 18, 2, LANES)
    flowed, line = flow(packed, halos(packed, count_t, count_z))
    loops = loops_of(line.reshape(2, 3, 3, 2, LANES), count_t)
    return flowed.reshape(links.shape), loops.reshape(2, 3, 3, 1, 2, LANES)


def solution(mesh):
    return jax.shard_map(
        local,
        mesh=mesh,
        in_specs=(P(None, None, None, None, "ta", "gz", None),),
        out_specs=(
            P(None, None, None, None, "ta", "gz", None),
            P(None, None, None, "ta", "gz", None),
        ),
        check_vma=False,
    )
```

```python
import jax
import jax.numpy as jnp
from jax import lax
from jax.experimental import pallas as pl
from jax.experimental.pallas import tpu as pltpu
from jax.sharding import PartitionSpec as P

LX = 8
LY = 16
LANES = LX * LY
MESH = pl.DeviceIdType.MESH


def factors(count):
    first = 4 if count % 4 == 0 and count > 8 else 2
    rest = count // first
    third = 4 if rest % 4 == 0 and rest > 4 else 2
    return first, rest // third, third


def entry(matrix, row, col, adjoint):
    if adjoint:
        return matrix[col * 3 + row], matrix[9 + col * 3 + row], -1
    return matrix[row * 3 + col], matrix[9 + row * 3 + col], 1


def tile_product(left, right, left_adjoint=False, right_adjoint=False):
    real, imag = [], []
    for row in range(3):
        for col in range(3):
            re = im = None
            for mid in range(3):
                a, b, s = entry(left, row, mid, left_adjoint)
                c, d, r = entry(right, mid, col, right_adjoint)
                ac, bd, ad, bc = a * c, b * d, a * d, b * c
                re_term = ac - bd if s * r > 0 else ac + bd
                re = re_term if re is None else re + re_term
                if im is None:
                    if r > 0:
                        im = ad + bc if s > 0 else ad - bc
                    else:
                        im = bc - ad if s > 0 else -(ad + bc)
                else:
                    im = im + ad if r > 0 else im - ad
                    im = im + bc if s > 0 else im - bc
            real.append(re)
            imag.append(im)
    return real + imag


def tile_helpers():
    group = lax.broadcasted_iota(jnp.int32, (8, LANES), 0) // 2
    y = lax.broadcasted_iota(jnp.int32, (8, LANES), 1) % LY

    def pick(tiles):
        rest = jnp.where(group == 2, tiles[2], tiles[3])
        return jnp.where(group == 0, tiles[0], jnp.where(group == 1, tiles[1], rest))

    def x_plus(tile):
        return pltpu.roll(tile, LANES - LY, 1)

    def x_minus(tile):
        return pltpu.roll(tile, LY, 1)

    def y_plus(tile):
        return jnp.where(
            y == LY - 1, pltpu.roll(tile, LY - 1, 1), pltpu.roll(tile, LANES - 1, 1)
        )

    def y_minus(tile):
        return jnp.where(
            y == 0, pltpu.roll(tile, LANES - LY + 1, 1), pltpu.roll(tile, 1, 1)
        )

    return group, pick, x_plus, x_minus, y_plus, y_minus


def plus_unity(matrix):
    return [v + 1.0 if i in (0, 4, 8) else v for i, v in enumerate(matrix)]


def flowed_link(link, total):
    omega = tile_product(link, total)
    trace = (omega[9] + omega[13] + omega[17]) * (1.0 / 3.0)
    generator = [None] * 18
    for row in range(3):
        for col in range(3):
            a, b = row * 3 + col, col * 3 + row
            generator[a] = -0.125 * (omega[a] - omega[b])
            part = 0.5 * (omega[9 + a] + omega[9 + b])
            if row == col:
                part = part - trace
            generator[9 + a] = -0.25 * part
    series = plus_unity([v * (1.0 / 6.0) for v in generator])
    for order in range(5, 0, -1):
        series = tile_product(generator, series)
        series = plus_unity([v * (1.0 / order) for v in series])
    return tile_product(series, link)


def both_staples(a, b, c, d, e, f):
    upper = tile_product(tile_product(a, b, False, True), c, False, True)
    lower = tile_product(tile_product(d, e, True, True), f)
    return [v + w for v, w in zip(upper, lower)]


def pack_own(u, pk):
    for i in range(18):
        for mu in range(4):
            pk[0, i, 2 * mu : 2 * mu + 2, :] = u[mu, i]


def flow_line(u, tp, cz, zm0, zm3, zp0, pk, sides, line):
    group, pick, x_plus, x_minus, y_plus, y_minus = tile_helpers()
    for i in range(18):
        for mu in range(1, 4):
            pk[1, i, 2 * mu : 2 * mu + 2, :] = tp[mu - 1, i]
        sides[0, i, 6:7, :] = u[0, i, 1:2]
        sides[0, i, 7:8, :] = zp0[0, i]
        sides[1, i, 6:7, :] = cz[0, i, 1:2]
        sides[1, i, 7:8, :] = tp[2, i, 0:1]
        sides[2, i, 6:7, :] = zm0[0, i]
        sides[2, i, 7:8, :] = u[0, i, 0:1]
        sides[3, i, 6:7, :] = zm3[0, i]
        sides[3, i, 7:8, :] = u[3, i, 0:1]
    first = group == 0

    def spread(tile):
        tile = tile + pltpu.roll(tile, 4, 0)
        return tile + pltpu.roll(tile, 2, 0)

    here = [pk[0, i] for i in range(18)]
    ahead = [pk[1, i] for i in range(18)]
    link = [spread(jnp.where(first, tile, 0.0)) for tile in here]
    side = [[sides[f, i] for i in range(18)] for f in range(4)]
    b = [pick([v, x_plus(v), y_plus(v), s]) for v, s in zip(link, side[0])]
    d = [pick([v, x_minus(v), y_minus(v), s]) for v, s in zip(ahead, side[1])]
    e = [pick([v, x_minus(v), y_minus(v), s]) for v, s in zip(link, side[2])]
    f = [pick([v, x_minus(v), y_minus(v), s]) for v, s in zip(here, side[3])]
    total = both_staples(ahead, b, here, d, e, f)
    total = [spread(jnp.where(first, 0.0, v)) for v in total]
    result = flowed_link(link, total)
    for i in range(18):
        line[i // 9, (i // 3) % 3, i % 3] = result[i][0:2]


def flow_all(u, tp, tm, cz, ct, zm0, zm12, zm3, zp0, zp12, pk, fields, result):
    group, pick, x_plus, x_minus, y_plus, y_minus = tile_helpers()
    for i in range(18):
        below = (zm0[0, i], zm12[0, i], zm12[1, i], zm3[0, i])
        above = (zp0[0, i], zp12[0, i], zp12[1, i])
        for mu in range(4):
            pk[2, i, 2 * mu : 2 * mu + 2, :] = tm[mu, i]
            pk[4, i, 2 * mu : 2 * mu + 1, :] = below[mu]
            pk[4, i, 2 * mu + 1 : 2 * mu + 2, :] = u[mu, i, 0:1]
            if mu < 3:
                pk[3, i, 2 * mu : 2 * mu + 1, :] = u[mu, i, 1:2]
                pk[3, i, 2 * mu + 1 : 2 * mu + 2, :] = above[mu]
        pk[5, i, 0:1, :] = tm[0, i, 1:2]
        pk[5, i, 1:2, :] = ct[0, i, 0:1]
        pk[5, i, 6:7, :] = cz[0, i, 1:2]
        pk[5, i, 7:8, :] = tp[2, i, 0:1]

    def lowered(tile, k):
        return pltpu.roll(tile, 8 - 2 * k, 0)

    def pack_fields(i):
        here, t_up, t_down, z_up, z_down, corner = (pk[f, i] for f in range(6))
        up = [t_up, x_plus(here), y_plus(here), z_up]
        down = [t_down, x_minus(here), y_minus(here), z_down]
        base = pick(down)
        t_side = [None, corner, y_plus(t_down), x_plus(t_down)]
        z_side = [None, y_plus(z_down), x_plus(z_down), corner]
        for k in range(1, 4):
            ahead = pick([up[(nu - k) % 4] for nu in range(4)])
            behind = pick([down[(nu - k) % 4] for nu in range(4)])
            cross = pick([t_side[k], x_minus(ahead), y_minus(ahead), z_side[k]])
            fields[0, k - 1, i] = lowered(ahead, k)
            fields[1, 3 - k, i] = ahead
            fields[2, k - 1, i] = lowered(here, k)
            fields[3, k - 1, i] = lowered(cross, k)
            fields[4, 3 - k, i] = behind
            fields[5, k - 1, i] = lowered(base, k)

    for i in range(18):
        pack_fields(i)
    total = None
    for k in range(3):
        mats = [[fields[field, k, i] for i in range(18)] for field in range(6)]
        both = both_staples(*mats)
        total = both if total is None else [a + b for a, b in zip(total, both)]
    flowed = flowed_link([pk[0, i] for i in range(18)], total)
    for i in range(18):
        result[i] = flowed[i]


def product(left, right):
    re = im = None
    for mid in range(3):
        a, b = left[0][:, mid : mid + 1], left[1][:, mid : mid + 1]
        c, d = right[0][mid : mid + 1], right[1][mid : mid + 1]
        re_term, im_term = a * c - b * d, a * d + b * c
        re = re_term if re is None else re + re_term
        im = im_term if im is None else im + im_term
    return re, im


def sweep_kernel(count_t, count_z, links, result, out, u, tp, tm, cz, ct, zm0, zm12, zm3, zp0, zp12,
                 pk, sides, fields, line, slots1, slots2, slots3, row_total, plane_total,
                 own_sem, halo_send, halo_recv, send, recv):
    t = lax.axis_index("ta")
    z = lax.axis_index("gz")
    t_next, t_prev = lax.rem(t + 1, count_t), lax.rem(t + count_t - 1, count_t)
    z_next, z_prev = lax.rem(z + 1, count_z), lax.rem(z + count_z - 1, count_z)
    sizes = factors(count_t)
    strides = (1, sizes[0], sizes[0] * sizes[1])
    digits = [lax.rem(t // stride, size) for stride, size in zip(strides, sizes)]
    slots = (slots1, slots2, slots3)

    def peer(stage, offset):
        size, stride, digit = sizes[stage], strides[stage], digits[stage]
        moved = lax.rem(digit + size - offset, size)
        return (t + (moved - digit) * stride, z)

    halo_peers = [
        (t_prev, z), (t_next, z), (t, z_next), (t, z_prev), (t_prev, z_next), (t_next, z_prev)
    ]
    peers = halo_peers + [peer(s, d) for s in range(3) for d in range(1, sizes[s])]
    barrier = pltpu.get_barrier_semaphore()
    for other in peers:
        pl.semaphore_signal(barrier, inc=1, device_id=other, device_id_type=MESH)
    own = pltpu.make_async_copy(links, u, own_sem)
    own.start()
    own.wait()
    pack_own(u, pk)
    pl.semaphore_wait(barrier, len(peers))

    def layer(first, size, row):
        return u.at[pl.ds(first, size), :, pl.ds(row, 1), :]

    plan = [
        (u.at[pl.ds(3, 1)], cz, (t_prev, z_next)),
        (layer(0, 1, 1), zm0, (t, z_next)),
        (layer(3, 1, 1), zm3, (t, z_next)),
        (layer(0, 1, 0), zp0, (t, z_prev)),
        (u.at[pl.ds(1, 3)], tp, (t_prev, z)),
        (u.at[pl.ds(0, 1)], ct, (t_next, z_prev)),
        (u, tm, (t_next, z)),
        (layer(1, 2, 1), zm12, (t, z_next)),
        (layer(1, 2, 0), zp12, (t, z_prev)),
    ]
    halos = [
        pltpu.make_async_remote_copy(
            src_ref=source,
            dst_ref=target,
            send_sem=halo_send.at[index],
            recv_sem=halo_recv.at[index],
            device_id=other,
            device_id_type=MESH,
        )
        for index, (source, target, other) in enumerate(plan)
    ]
    for copy in halos[:7]:
        copy.start()
    for copy in halos[:5]:
        copy.wait_recv()
    for copy in halos[7:]:
        copy.start()
    flow_line(u, tp, cz, zm0, zm3, zp0, pk, sides, line)

    shape = (3, 3) + line.shape[-2:]
    diagonal = [
        [jnp.full(shape[2:], 1.0 if a == b else 0.0, jnp.float32) for b in range(3)]
        for a in range(3)
    ]
    unity = jnp.stack([jnp.stack(row) for row in diagonal])
    nought = jnp.zeros(shape, jnp.float32)
    start = [0, sizes[0] - 1, sizes[0] + sizes[1] - 2]

    def share(stage, source):
        copies = []
        for offset in range(1, sizes[stage]):
            index = start[stage] + offset - 1
            copies.append(
                pltpu.make_async_remote_copy(
                    src_ref=source,
                    dst_ref=slots[stage].at[offset - 1],
                    send_sem=send.at[index],
                    recv_sem=recv.at[index],
                    device_id=peer(stage, offset),
                    device_id_type=MESH,
                )
            )
        for copy in copies:
            copy.start()
        return copies

    def ordered(stage, copies):
        after = before = None
        for offset in range(1, sizes[stage]):
            copies[offset - 1].wait_recv()
            re, im = slots[stage][offset - 1, 0], slots[stage][offset - 1, 1]
            inside = digits[stage] + offset < sizes[stage]
            high = (jnp.where(inside, re, unity), jnp.where(inside, im, nought))
            low = (jnp.where(inside, unity, re), jnp.where(inside, nought, im))
            after = high if after is None else product(after, high)
            before = low if before is None else product(before, low)
        return after, before

    copies1 = share(0, line)
    row_after, row_before = ordered(0, copies1)
    row_after = product((line[0], line[1]), row_after)
    row = product(row_before, row_after)
    row_total[0], row_total[1] = row
    copies2 = share(1, row_total)
    for copy in halos[5:]:
        copy.wait_recv()
    flow_all(u, tp, tm, cz, ct, zm0, zm12, zm3, zp0, zp12, pk, fields, result)
    plane_after, plane_before = ordered(1, copies2)
    plane = product(plane_before, product(row, plane_after))
    plane_total[0], plane_total[1] = plane
    copies3 = share(2, plane_total)
    left = product(row_after, plane_after)
    right = product(plane_before, row_before)
    for offset in range(1, sizes[2]):
        copies3[offset - 1].wait_recv()
        left = product(left, (slots3[offset - 1, 0], slots3[offset - 1, 1]))
    out[0], out[1] = product(left, right)
    for copy in halos + copies1 + copies2 + copies3:
        copy.wait_send()


def sweep(links, count_t, count_z):
    sizes = factors(count_t)
    messages = sum(sizes) - 3
    matrix = (2, 3, 3, 2, LANES)

    def space(*shape):
        return pltpu.VMEM(shape, jnp.float32)

    vmem = pl.BlockSpec(memory_space=pltpu.VMEM)
    return pl.pallas_call(
        lambda *refs: sweep_kernel(count_t, count_z, *refs),
        out_shape=[
            jax.ShapeDtypeStruct((18, 8, LANES), jnp.float32),
            jax.ShapeDtypeStruct(matrix, jnp.float32),
        ],
        in_specs=[pl.BlockSpec(memory_space=pl.ANY)],
        out_specs=[vmem] * 2,
        scratch_shapes=[
            space(4, 18, 2, LANES),
            space(3, 18, 2, LANES),
            space(4, 18, 2, LANES),
            space(1, 18, 2, LANES),
            space(1, 18, 2, LANES),
            space(1, 18, 1, LANES),
            space(2, 18, 1, LANES),
            space(1, 18, 1, LANES),
            space(1, 18, 1, LANES),
            space(2, 18, 1, LANES),
            space(6, 18, 8, LANES),
            space(4, 18, 8, LANES),
            space(6, 3, 18, 8, LANES),
            space(*matrix),
            space(sizes[0] - 1, *matrix),
            space(sizes[1] - 1, *matrix),
            space(sizes[2] - 1, *matrix),
            space(*matrix),
            space(*matrix),
            pltpu.SemaphoreType.DMA,
            pltpu.SemaphoreType.DMA((9,)),
            pltpu.SemaphoreType.DMA((9,)),
            pltpu.SemaphoreType.DMA((messages,)),
            pltpu.SemaphoreType.DMA((messages,)),
        ],
        compiler_params=pltpu.CompilerParams(collective_id=0, has_side_effects=True),
        name="halo_flow_loops",
    )(links)


def unpack_kernel(packed, product_in, flowed, loops):
    for i in range(18):
        for mu in range(4):
            flowed[mu, i] = packed[i, 2 * mu : 2 * mu + 2, :]
    loops[...] = product_in[...]


def unpacked(packed, loops):
    vmem = pl.BlockSpec(memory_space=pltpu.VMEM)
    return pl.pallas_call(
        unpack_kernel,
        out_shape=[
            jax.ShapeDtypeStruct((4, 18, 2, LANES), jnp.float32),
            jax.ShapeDtypeStruct(loops.shape, jnp.float32),
        ],
        in_specs=[vmem] * 2,
        out_specs=[vmem] * 2,
        name="unpack",
    )(packed, loops)


def local(links):
    count_t, count_z = lax.axis_size("ta"), lax.axis_size("gz")
    packed, loops = sweep(links.reshape(4, 18, 2, LANES), count_t, count_z)
    flowed, loops = unpacked(packed, loops)
    return flowed.reshape(links.shape), loops.reshape(2, 3, 3, 1, 2, LANES)


def solution(mesh):
    return jax.shard_map(
        local,
        mesh=mesh,
        in_specs=(P(None, None, None, None, "ta", "gz", None),),
        out_specs=(
            P(None, None, None, None, "ta", "gz", None),
            P(None, None, None, "ta", "gz", None),
        ),
        check_vma=False,
    )
```

```python
import jax
import jax.numpy as jnp
from jax import lax
from jax.experimental import pallas as pl
from jax.experimental.pallas import tpu as pltpu
from jax.sharding import PartitionSpec as P

LX = 8
LY = 16
LANES = LX * LY
MESH = pl.DeviceIdType.MESH


def factors(count):
    first = 4 if count % 4 == 0 and count > 8 else 2
    rest = count // first
    third = 4 if rest % 4 == 0 and rest > 4 else 2
    return first, rest // third, third


def entry(matrix, row, col, adjoint):
    if adjoint:
        return matrix[col * 3 + row], matrix[9 + col * 3 + row], -1
    return matrix[row * 3 + col], matrix[9 + row * 3 + col], 1


def tile_product(left, right, left_adjoint=False, right_adjoint=False):
    real, imag = [], []
    for row in range(3):
        for col in range(3):
            re = im = None
            for mid in range(3):
                a, b, s = entry(left, row, mid, left_adjoint)
                c, d, r = entry(right, mid, col, right_adjoint)
                ac, bd, ad, bc = a * c, b * d, a * d, b * c
                re_term = ac - bd if s * r > 0 else ac + bd
                re = re_term if re is None else re + re_term
                if im is None:
                    if r > 0:
                        im = ad + bc if s > 0 else ad - bc
                    else:
                        im = bc - ad if s > 0 else -(ad + bc)
                else:
                    im = im + ad if r > 0 else im - ad
                    im = im + bc if s > 0 else im - bc
            real.append(re)
            imag.append(im)
    return real + imag


def tile_helpers():
    group = lax.broadcasted_iota(jnp.int32, (8, LANES), 0) // 2
    y = lax.broadcasted_iota(jnp.int32, (8, LANES), 1) % LY

    def pick(tiles):
        rest = jnp.where(group == 2, tiles[2], tiles[3])
        return jnp.where(group == 0, tiles[0], jnp.where(group == 1, tiles[1], rest))

    def x_plus(tile):
        return pltpu.roll(tile, LANES - LY, 1)

    def x_minus(tile):
        return pltpu.roll(tile, LY, 1)

    def y_plus(tile):
        return jnp.where(
            y == LY - 1, pltpu.roll(tile, LY - 1, 1), pltpu.roll(tile, LANES - 1, 1)
        )

    def y_minus(tile):
        return jnp.where(
            y == 0, pltpu.roll(tile, LANES - LY + 1, 1), pltpu.roll(tile, 1, 1)
        )

    return group, pick, x_plus, x_minus, y_plus, y_minus


def plus_unity(matrix):
    return [v + 1.0 if i in (0, 4, 8) else v for i, v in enumerate(matrix)]


def flowed_link(link, total):
    omega = tile_product(link, total)
    trace = (omega[9] + omega[13] + omega[17]) * (1.0 / 3.0)
    generator = [None] * 18
    for row in range(3):
        for col in range(3):
            a, b = row * 3 + col, col * 3 + row
            generator[a] = -0.125 * (omega[a] - omega[b])
            part = 0.5 * (omega[9 + a] + omega[9 + b])
            if row == col:
                part = part - trace
            generator[9 + a] = -0.25 * part
    series = plus_unity([v * (1.0 / 6.0) for v in generator])
    for order in range(5, 0, -1):
        series = tile_product(generator, series)
        series = plus_unity([v * (1.0 / order) for v in series])
    return tile_product(series, link)


def both_staples(a, b, c, d, e, f):
    upper = tile_product(tile_product(a, b, False, True), c, False, True)
    lower = tile_product(tile_product(d, e, True, True), f)
    return [v + w for v, w in zip(upper, lower)]


def pack_own(u, pk):
    for i in range(18):
        for mu in range(4):
            pk[0, i, 2 * mu : 2 * mu + 2, :] = u[mu, i]


def flow_line(u, tp, cz, zm0, zm3, zp0, pk, sides, line):
    group, pick, x_plus, x_minus, y_plus, y_minus = tile_helpers()
    for i in range(18):
        for mu in range(1, 4):
            pk[1, i, 2 * mu : 2 * mu + 2, :] = tp[mu - 1, i]
        sides[0, i, 6:7, :] = u[0, i, 1:2]
        sides[0, i, 7:8, :] = zp0[0, i]
        sides[1, i, 6:7, :] = cz[0, i, 1:2]
        sides[1, i, 7:8, :] = tp[2, i, 0:1]
        sides[2, i, 6:7, :] = zm0[0, i]
        sides[2, i, 7:8, :] = u[0, i, 0:1]
        sides[3, i, 6:7, :] = zm3[0, i]
        sides[3, i, 7:8, :] = u[3, i, 0:1]
    first = group == 0

    def spread(tile):
        tile = tile + pltpu.roll(tile, 4, 0)
        return tile + pltpu.roll(tile, 2, 0)

    here = [pk[0, i] for i in range(18)]
    ahead = [pk[1, i] for i in range(18)]
    link = [spread(jnp.where(first, tile, 0.0)) for tile in here]
    side = [[sides[f, i] for i in range(18)] for f in range(4)]
    b = [pick([v, x_plus(v), y_plus(v), s]) for v, s in zip(link, side[0])]
    d = [pick([v, x_minus(v), y_minus(v), s]) for v, s in zip(ahead, side[1])]
    e = [pick([v, x_minus(v), y_minus(v), s]) for v, s in zip(link, side[2])]
    f = [pick([v, x_minus(v), y_minus(v), s]) for v, s in zip(here, side[3])]
    total = both_staples(ahead, b, here, d, e, f)
    total = [spread(jnp.where(first, 0.0, v)) for v in total]
    result = flowed_link(link, total)
    for i in range(18):
        line[i // 9, (i // 3) % 3, i % 3] = result[i][0:2]


def flow_all(u, tp, tm, cz, ct, zm0, zm12, zm3, zp0, zp12, pk, fields, result):
    group, pick, x_plus, x_minus, y_plus, y_minus = tile_helpers()
    for i in range(18):
        below = (zm0[0, i], zm12[0, i], zm12[1, i], zm3[0, i])
        above = (zp0[0, i], zp12[0, i], zp12[1, i])
        for mu in range(4):
            pk[2, i, 2 * mu : 2 * mu + 2, :] = tm[mu, i]
            pk[4, i, 2 * mu : 2 * mu + 1, :] = below[mu]
            pk[4, i, 2 * mu + 1 : 2 * mu + 2, :] = u[mu, i, 0:1]
            if mu < 3:
                pk[3, i, 2 * mu : 2 * mu + 1, :] = u[mu, i, 1:2]
                pk[3, i, 2 * mu + 1 : 2 * mu + 2, :] = above[mu]
        pk[5, i, 0:1, :] = tm[0, i, 1:2]
        pk[5, i, 1:2, :] = ct[0, i, 0:1]
        pk[5, i, 6:7, :] = cz[0, i, 1:2]
        pk[5, i, 7:8, :] = tp[2, i, 0:1]

    def lowered(tile, k):
        return pltpu.roll(tile, 8 - 2 * k, 0)

    def pack_fields(i):
        here, t_up, t_down, z_up, z_down, corner = (pk[f, i] for f in range(6))
        up = [t_up, x_plus(here), y_plus(here), z_up]
        down = [t_down, x_minus(here), y_minus(here), z_down]
        base = pick(down)
        t_side = [None, corner, y_plus(t_down), x_plus(t_down)]
        z_side = [None, y_plus(z_down), x_plus(z_down), corner]
        for k in range(1, 4):
            ahead = pick([up[(nu - k) % 4] for nu in range(4)])
            behind = pick([down[(nu - k) % 4] for nu in range(4)])
            cross = pick([t_side[k], x_minus(ahead), y_minus(ahead), z_side[k]])
            fields[0, k - 1, i] = lowered(ahead, k)
            fields[1, 3 - k, i] = ahead
            fields[2, k - 1, i] = lowered(here, k)
            fields[3, k - 1, i] = lowered(cross, k)
            fields[4, 3 - k, i] = behind
            fields[5, k - 1, i] = lowered(base, k)

    for i in range(18):
        pack_fields(i)
    total = None
    for k in range(3):
        mats = [[fields[field, k, i] for i in range(18)] for field in range(6)]
        both = both_staples(*mats)
        total = both if total is None else [a + b for a, b in zip(total, both)]
    flowed = flowed_link([pk[0, i] for i in range(18)], total)
    for i in range(18):
        result[i] = flowed[i]


def product(left, right):
    re = im = None
    for mid in range(3):
        a, b = left[0][:, mid : mid + 1], left[1][:, mid : mid + 1]
        c, d = right[0][mid : mid + 1], right[1][mid : mid + 1]
        re_term, im_term = a * c - b * d, a * d + b * c
        re = re_term if re is None else re + re_term
        im = im_term if im is None else im + im_term
    return re, im


def sweep_kernel(count_t, count_z, links, result, out, u, tp, tm, cz, ct, zm0, zm12, zm3, zp0, zp12,
                 pk, sides, fields, line, slots1, slots2, slots3, row_total, plane_total,
                 own_sem, halo_send, halo_recv, send, recv):
    t = lax.axis_index("ta")
    z = lax.axis_index("gz")
    t_next, t_prev = lax.rem(t + 1, count_t), lax.rem(t + count_t - 1, count_t)
    z_next, z_prev = lax.rem(z + 1, count_z), lax.rem(z + count_z - 1, count_z)
    sizes = factors(count_t)
    strides = (1, sizes[0], sizes[0] * sizes[1])
    digits = [lax.rem(t // stride, size) for stride, size in zip(strides, sizes)]
    slots = (slots1, slots2, slots3)

    def peer(stage, offset):
        size, stride, digit = sizes[stage], strides[stage], digits[stage]
        moved = lax.rem(digit + size - offset, size)
        return (t + (moved - digit) * stride, z)

    halo_peers = [
        (t_prev, z), (t_next, z), (t, z_next), (t, z_prev), (t_prev, z_next), (t_next, z_prev)
    ]
    peers = halo_peers + [peer(s, d) for s in range(3) for d in range(1, sizes[s])]
    barrier = pltpu.get_barrier_semaphore()
    for other in peers:
        pl.semaphore_signal(barrier, inc=1, device_id=other, device_id_type=MESH)
    own = pltpu.make_async_copy(links, u, own_sem)
    own.start()
    pl.semaphore_wait(barrier, len(peers))

    def layer(first, size, row):
        return links.at[pl.ds(first, size), :, pl.ds(row, 1), :]

    plan = [
        (links.at[pl.ds(3, 1)], cz, (t_prev, z_next)),
        (layer(0, 1, 1), zm0, (t, z_next)),
        (layer(3, 1, 1), zm3, (t, z_next)),
        (layer(0, 1, 0), zp0, (t, z_prev)),
        (links.at[pl.ds(1, 3)], tp, (t_prev, z)),
        (links.at[pl.ds(0, 1)], ct, (t_next, z_prev)),
        (links, tm, (t_next, z)),
        (layer(1, 2, 1), zm12, (t, z_next)),
        (layer(1, 2, 0), zp12, (t, z_prev)),
    ]
    halos = [
        pltpu.make_async_remote_copy(
            src_ref=source,
            dst_ref=target,
            send_sem=halo_send.at[index],
            recv_sem=halo_recv.at[index],
            device_id=other,
            device_id_type=MESH,
        )
        for index, (source, target, other) in enumerate(plan)
    ]
    for copy in halos[:7]:
        copy.start()
    own.wait()
    pack_own(u, pk)
    for copy in halos[:5]:
        copy.wait_recv()
    for copy in halos[7:]:
        copy.start()
    flow_line(u, tp, cz, zm0, zm3, zp0, pk, sides, line)

    shape = (3, 3) + line.shape[-2:]
    diagonal = [
        [jnp.full(shape[2:], 1.0 if a == b else 0.0, jnp.float32) for b in range(3)]
        for a in range(3)
    ]
    unity = jnp.stack([jnp.stack(row) for row in diagonal])
    nought = jnp.zeros(shape, jnp.float32)
    start = [0, sizes[0] - 1, sizes[0] + sizes[1] - 2]

    def share(stage, source):
        copies = []
        for offset in range(1, sizes[stage]):
            index = start[stage] + offset - 1
            copies.append(
                pltpu.make_async_remote_copy(
                    src_ref=source,
                    dst_ref=slots[stage].at[offset - 1],
                    send_sem=send.at[index],
                    recv_sem=recv.at[index],
                    device_id=peer(stage, offset),
                    device_id_type=MESH,
                )
            )
        for copy in copies:
            copy.start()
        return copies

    def ordered(stage, copies):
        after = before = None
        for offset in range(1, sizes[stage]):
            copies[offset - 1].wait_recv()
            re, im = slots[stage][offset - 1, 0], slots[stage][offset - 1, 1]
            inside = digits[stage] + offset < sizes[stage]
            high = (jnp.where(inside, re, unity), jnp.where(inside, im, nought))
            low = (jnp.where(inside, unity, re), jnp.where(inside, nought, im))
            after = high if after is None else product(after, high)
            before = low if before is None else product(before, low)
        return after, before

    copies1 = share(0, line)
    row_after, row_before = ordered(0, copies1)
    row_after = product((line[0], line[1]), row_after)
    row = product(row_before, row_after)
    row_total[0], row_total[1] = row
    copies2 = share(1, row_total)
    plane_after, plane_before = ordered(1, copies2)
    plane = product(plane_before, product(row, plane_after))
    plane_total[0], plane_total[1] = plane
    copies3 = share(2, plane_total)
    left = product(row_after, plane_after)
    right = product(plane_before, row_before)
    for copy in halos[5:]:
        copy.wait_recv()
    flow_all(u, tp, tm, cz, ct, zm0, zm12, zm3, zp0, zp12, pk, fields, result)
    for offset in range(1, sizes[2]):
        copies3[offset - 1].wait_recv()
        left = product(left, (slots3[offset - 1, 0], slots3[offset - 1, 1]))
    out[0], out[1] = product(left, right)
    for copy in halos + copies1 + copies2 + copies3:
        copy.wait_send()


def sweep(links, count_t, count_z):
    sizes = factors(count_t)
    messages = sum(sizes) - 3
    matrix = (2, 3, 3, 2, LANES)

    def space(*shape):
        return pltpu.VMEM(shape, jnp.float32)

    vmem = pl.BlockSpec(memory_space=pltpu.VMEM)
    return pl.pallas_call(
        lambda *refs: sweep_kernel(count_t, count_z, *refs),
        out_shape=[
            jax.ShapeDtypeStruct((18, 8, LANES), jnp.float32),
            jax.ShapeDtypeStruct(matrix, jnp.float32),
        ],
        in_specs=[pl.BlockSpec(memory_space=pl.ANY)],
        out_specs=[vmem] * 2,
        scratch_shapes=[
            space(4, 18, 2, LANES),
            space(3, 18, 2, LANES),
            space(4, 18, 2, LANES),
            space(1, 18, 2, LANES),
            space(1, 18, 2, LANES),
            space(1, 18, 1, LANES),
            space(2, 18, 1, LANES),
            space(1, 18, 1, LANES),
            space(1, 18, 1, LANES),
            space(2, 18, 1, LANES),
            space(6, 18, 8, LANES),
            space(4, 18, 8, LANES),
            space(6, 3, 18, 8, LANES),
            space(*matrix),
            space(sizes[0] - 1, *matrix),
            space(sizes[1] - 1, *matrix),
            space(sizes[2] - 1, *matrix),
            space(*matrix),
            space(*matrix),
            pltpu.SemaphoreType.DMA,
            pltpu.SemaphoreType.DMA((9,)),
            pltpu.SemaphoreType.DMA((9,)),
            pltpu.SemaphoreType.DMA((messages,)),
            pltpu.SemaphoreType.DMA((messages,)),
        ],
        compiler_params=pltpu.CompilerParams(collective_id=0, has_side_effects=True),
        name="halo_flow_loops",
    )(links)


def unpack_kernel(packed, product_in, flowed, loops):
    for i in range(18):
        for mu in range(4):
            flowed[mu, i] = packed[i, 2 * mu : 2 * mu + 2, :]
    loops[...] = product_in[...]


def unpacked(packed, loops):
    vmem = pl.BlockSpec(memory_space=pltpu.VMEM)
    return pl.pallas_call(
        unpack_kernel,
        out_shape=[
            jax.ShapeDtypeStruct((4, 18, 2, LANES), jnp.float32),
            jax.ShapeDtypeStruct(loops.shape, jnp.float32),
        ],
        in_specs=[vmem] * 2,
        out_specs=[vmem] * 2,
        name="unpack",
    )(packed, loops)


def local(links):
    count_t, count_z = lax.axis_size("ta"), lax.axis_size("gz")
    packed, loops = sweep(links.reshape(4, 18, 2, LANES), count_t, count_z)
    flowed, loops = unpacked(packed, loops)
    return flowed.reshape(links.shape), loops.reshape(2, 3, 3, 1, 2, LANES)


def solution(mesh):
    return jax.shard_map(
        local,
        mesh=mesh,
        in_specs=(P(None, None, None, None, "ta", "gz", None),),
        out_specs=(
            P(None, None, None, None, "ta", "gz", None),
            P(None, None, None, "ta", "gz", None),
        ),
        check_vma=False,
    )
```

```python
import jax
import jax.numpy as jnp
from jax import lax
from jax.experimental import pallas as pl
from jax.experimental.pallas import tpu as pltpu
from jax.sharding import PartitionSpec as P

LX = 8
LY = 16
LANES = LX * LY
MESH = pl.DeviceIdType.MESH


def factors(count):
    first = 4 if count % 4 == 0 and count > 8 else 2
    rest = count // first
    third = 4 if rest % 4 == 0 and rest > 4 else 2
    return first, rest // third, third


def entry(matrix, row, col, adjoint):
    if adjoint:
        return matrix[col * 3 + row], matrix[9 + col * 3 + row], -1
    return matrix[row * 3 + col], matrix[9 + row * 3 + col], 1


def tile_product(left, right, left_adjoint=False, right_adjoint=False):
    real, imag = [], []
    for row in range(3):
        for col in range(3):
            re = im = None
            for mid in range(3):
                a, b, s = entry(left, row, mid, left_adjoint)
                c, d, r = entry(right, mid, col, right_adjoint)
                ac, bd, ad, bc = a * c, b * d, a * d, b * c
                re_term = ac - bd if s * r > 0 else ac + bd
                re = re_term if re is None else re + re_term
                if im is None:
                    if r > 0:
                        im = ad + bc if s > 0 else ad - bc
                    else:
                        im = bc - ad if s > 0 else -(ad + bc)
                else:
                    im = im + ad if r > 0 else im - ad
                    im = im + bc if s > 0 else im - bc
            real.append(re)
            imag.append(im)
    return real + imag


def tile_helpers():
    group = lax.broadcasted_iota(jnp.int32, (8, LANES), 0) // 2
    y = lax.broadcasted_iota(jnp.int32, (8, LANES), 1) % LY

    def pick(tiles):
        rest = jnp.where(group == 2, tiles[2], tiles[3])
        return jnp.where(group == 0, tiles[0], jnp.where(group == 1, tiles[1], rest))

    def x_plus(tile):
        return pltpu.roll(tile, LANES - LY, 1)

    def x_minus(tile):
        return pltpu.roll(tile, LY, 1)

    def y_plus(tile):
        return jnp.where(
            y == LY - 1, pltpu.roll(tile, LY - 1, 1), pltpu.roll(tile, LANES - 1, 1)
        )

    def y_minus(tile):
        return jnp.where(
            y == 0, pltpu.roll(tile, LANES - LY + 1, 1), pltpu.roll(tile, 1, 1)
        )

    return group, pick, x_plus, x_minus, y_plus, y_minus


def plus_unity(matrix):
    return [v + 1.0 if i in (0, 4, 8) else v for i, v in enumerate(matrix)]


def flowed_link(link, total):
    omega = tile_product(link, total)
    trace = (omega[9] + omega[13] + omega[17]) * (1.0 / 3.0)
    generator = [None] * 18
    for row in range(3):
        for col in range(3):
            a, b = row * 3 + col, col * 3 + row
            generator[a] = -0.125 * (omega[a] - omega[b])
            part = 0.5 * (omega[9 + a] + omega[9 + b])
            if row == col:
                part = part - trace
            generator[9 + a] = -0.25 * part
    series = plus_unity([v * (1.0 / 6.0) for v in generator])
    for order in range(5, 0, -1):
        series = tile_product(generator, series)
        series = plus_unity([v * (1.0 / order) for v in series])
    return tile_product(series, link)


def both_staples(a, b, c, d, e, f):
    upper = tile_product(tile_product(a, b, False, True), c, False, True)
    lower = tile_product(tile_product(d, e, True, True), f)
    return [v + w for v, w in zip(upper, lower)]


def pack_own(u, pk):
    for i in range(18):
        for mu in range(4):
            pk[0, i, 2 * mu : 2 * mu + 2, :] = u[mu, i]


def flow_line(u, tp, cz, zm0, zm3, zp0, pk, sides, line):
    group, pick, x_plus, x_minus, y_plus, y_minus = tile_helpers()
    for i in range(18):
        for mu in range(1, 4):
            pk[1, i, 2 * mu : 2 * mu + 2, :] = tp[mu - 1, i]
        sides[0, i, 6:7, :] = u[0, i, 1:2]
        sides[0, i, 7:8, :] = zp0[0, i]
        sides[1, i, 6:7, :] = cz[0, i]
        sides[1, i, 7:8, :] = tp[2, i, 0:1]
        sides[2, i, 6:7, :] = zm0[0, i]
        sides[2, i, 7:8, :] = u[0, i, 0:1]
        sides[3, i, 6:7, :] = zm3[0, i]
        sides[3, i, 7:8, :] = u[3, i, 0:1]
    first = group == 0

    def spread(tile):
        tile = tile + pltpu.roll(tile, 4, 0)
        return tile + pltpu.roll(tile, 2, 0)

    here = [pk[0, i] for i in range(18)]
    ahead = [pk[1, i] for i in range(18)]
    link = [spread(jnp.where(first, tile, 0.0)) for tile in here]
    side = [[sides[f, i] for i in range(18)] for f in range(4)]
    b = [pick([v, x_plus(v), y_plus(v), s]) for v, s in zip(link, side[0])]
    d = [pick([v, x_minus(v), y_minus(v), s]) for v, s in zip(ahead, side[1])]
    e = [pick([v, x_minus(v), y_minus(v), s]) for v, s in zip(link, side[2])]
    f = [pick([v, x_minus(v), y_minus(v), s]) for v, s in zip(here, side[3])]
    total = both_staples(ahead, b, here, d, e, f)
    total = [spread(jnp.where(first, 0.0, v)) for v in total]
    result = flowed_link(link, total)
    for i in range(18):
        line[i // 9, (i // 3) % 3, i % 3] = result[i][0:2]


def flow_all(u, tp, tm, cz, ct, zm0, zm12, zm3, zp0, zp12, pk, fields, result):
    group, pick, x_plus, x_minus, y_plus, y_minus = tile_helpers()
    for i in range(18):
        below = (zm0[0, i], zm12[0, i], zm12[1, i], zm3[0, i])
        above = (zp0[0, i], zp12[0, i], zp12[1, i])
        for mu in range(4):
            pk[2, i, 2 * mu : 2 * mu + 2, :] = tm[mu, i]
            pk[4, i, 2 * mu : 2 * mu + 1, :] = below[mu]
            pk[4, i, 2 * mu + 1 : 2 * mu + 2, :] = u[mu, i, 0:1]
            if mu < 3:
                pk[3, i, 2 * mu : 2 * mu + 1, :] = u[mu, i, 1:2]
                pk[3, i, 2 * mu + 1 : 2 * mu + 2, :] = above[mu]
        pk[5, i, 0:1, :] = tm[0, i, 1:2]
        pk[5, i, 1:2, :] = ct[0, i]
        pk[5, i, 6:7, :] = cz[0, i]
        pk[5, i, 7:8, :] = tp[2, i, 0:1]

    def lowered(tile, k):
        return pltpu.roll(tile, 8 - 2 * k, 0)

    def pack_fields(i):
        here, t_up, t_down, z_up, z_down, corner = (pk[f, i] for f in range(6))
        up = [t_up, x_plus(here), y_plus(here), z_up]
        down = [t_down, x_minus(here), y_minus(here), z_down]
        base = pick(down)
        t_side = [None, corner, y_plus(t_down), x_plus(t_down)]
        z_side = [None, y_plus(z_down), x_plus(z_down), corner]
        for k in range(1, 4):
            ahead = pick([up[(nu - k) % 4] for nu in range(4)])
            behind = pick([down[(nu - k) % 4] for nu in range(4)])
            cross = pick([t_side[k], x_minus(ahead), y_minus(ahead), z_side[k]])
            fields[0, k - 1, i] = lowered(ahead, k)
            fields[1, 3 - k, i] = ahead
            fields[2, k - 1, i] = lowered(here, k)
            fields[3, k - 1, i] = lowered(cross, k)
            fields[4, 3 - k, i] = behind
            fields[5, k - 1, i] = lowered(base, k)

    for i in range(18):
        pack_fields(i)
    total = None
    for k in range(3):
        mats = [[fields[field, k, i] for i in range(18)] for field in range(6)]
        both = both_staples(*mats)
        total = both if total is None else [a + b for a, b in zip(total, both)]
    flowed = flowed_link([pk[0, i] for i in range(18)], total)
    for i in range(18):
        result[i] = flowed[i]


def product(left, right):
    re = im = None
    for mid in range(3):
        a, b = left[0][:, mid : mid + 1], left[1][:, mid : mid + 1]
        c, d = right[0][mid : mid + 1], right[1][mid : mid + 1]
        re_term, im_term = a * c - b * d, a * d + b * c
        re = re_term if re is None else re + re_term
        im = im_term if im is None else im + im_term
    return re, im


def sweep_kernel(count_t, count_z, links, result, out, u, tp, tm, cz, ct, zm0, zm12, zm3, zp0, zp12,
                 pk, sides, fields, line, slots1, slots2, slots3, row_total, plane_total,
                 own_sem, halo_send, halo_recv, send, recv):
    t = lax.axis_index("ta")
    z = lax.axis_index("gz")
    t_next, t_prev = lax.rem(t + 1, count_t), lax.rem(t + count_t - 1, count_t)
    z_next, z_prev = lax.rem(z + 1, count_z), lax.rem(z + count_z - 1, count_z)
    sizes = factors(count_t)
    strides = (1, sizes[0], sizes[0] * sizes[1])
    digits = [lax.rem(t // stride, size) for stride, size in zip(strides, sizes)]
    slots = (slots1, slots2, slots3)

    def peer(stage, offset):
        size, stride, digit = sizes[stage], strides[stage], digits[stage]
        moved = lax.rem(digit + size - offset, size)
        return (t + (moved - digit) * stride, z)

    halo_peers = [
        (t_prev, z), (t_next, z), (t, z_next), (t, z_prev), (t_prev, z_next), (t_next, z_prev)
    ]
    peers = halo_peers + [peer(s, d) for s in range(3) for d in range(1, sizes[s])]
    barrier = pltpu.get_barrier_semaphore()
    for other in peers:
        pl.semaphore_signal(barrier, inc=1, device_id=other, device_id_type=MESH)
    own = pltpu.make_async_copy(links, u, own_sem)
    own.start()
    pl.semaphore_wait(barrier, len(peers))

    def layer(first, size, row):
        return links.at[pl.ds(first, size), :, pl.ds(row, 1), :]

    plan = [
        (layer(3, 1, 1), cz, (t_prev, z_next)),
        (layer(0, 1, 1), zm0, (t, z_next)),
        (layer(3, 1, 1), zm3, (t, z_next)),
        (layer(0, 1, 0), zp0, (t, z_prev)),
        (links.at[pl.ds(1, 3)], tp, (t_prev, z)),
        (layer(0, 1, 0), ct, (t_next, z_prev)),
        (links, tm, (t_next, z)),
        (layer(1, 2, 1), zm12, (t, z_next)),
        (layer(1, 2, 0), zp12, (t, z_prev)),
    ]
    halos = [
        pltpu.make_async_remote_copy(
            src_ref=source,
            dst_ref=target,
            send_sem=halo_send.at[index],
            recv_sem=halo_recv.at[index],
            device_id=other,
            device_id_type=MESH,
        )
        for index, (source, target, other) in enumerate(plan)
    ]
    for copy in halos[:7]:
        copy.start()
    own.wait()
    pack_own(u, pk)
    for copy in halos[:5]:
        copy.wait_recv()
    for copy in halos[7:]:
        copy.start()
    flow_line(u, tp, cz, zm0, zm3, zp0, pk, sides, line)

    shape = (3, 3) + line.shape[-2:]
    diagonal = [
        [jnp.full(shape[2:], 1.0 if a == b else 0.0, jnp.float32) for b in range(3)]
        for a in range(3)
    ]
    unity = jnp.stack([jnp.stack(row) for row in diagonal])
    nought = jnp.zeros(shape, jnp.float32)
    start = [0, sizes[0] - 1, sizes[0] + sizes[1] - 2]

    def share(stage, source):
        copies = []
        for offset in range(1, sizes[stage]):
            index = start[stage] + offset - 1
            copies.append(
                pltpu.make_async_remote_copy(
                    src_ref=source,
                    dst_ref=slots[stage].at[offset - 1],
                    send_sem=send.at[index],
                    recv_sem=recv.at[index],
                    device_id=peer(stage, offset),
                    device_id_type=MESH,
                )
            )
        size = sizes[stage]
        for offset in sorted(range(1, size), key=lambda d: -min(d, size - d)):
            copies[offset - 1].start()
        return copies

    def ordered(stage, copies):
        after = before = None
        for offset in range(1, sizes[stage]):
            copies[offset - 1].wait_recv()
            re, im = slots[stage][offset - 1, 0], slots[stage][offset - 1, 1]
            inside = digits[stage] + offset < sizes[stage]
            high = (jnp.where(inside, re, unity), jnp.where(inside, im, nought))
            low = (jnp.where(inside, unity, re), jnp.where(inside, nought, im))
            after = high if after is None else product(after, high)
            before = low if before is None else product(before, low)
        return after, before

    copies1 = share(0, line)
    row_after, row_before = ordered(0, copies1)
    row_after = product((line[0], line[1]), row_after)
    row = product(row_before, row_after)
    row_total[0], row_total[1] = row
    copies2 = share(1, row_total)
    plane_after, plane_before = ordered(1, copies2)
    plane = product(plane_before, product(row, plane_after))
    plane_total[0], plane_total[1] = plane
    copies3 = share(2, plane_total)
    left = product(row_after, plane_after)
    right = product(plane_before, row_before)
    for copy in halos[5:]:
        copy.wait_recv()
    flow_all(u, tp, tm, cz, ct, zm0, zm12, zm3, zp0, zp12, pk, fields, result)
    for offset in range(1, sizes[2]):
        copies3[offset - 1].wait_recv()
        left = product(left, (slots3[offset - 1, 0], slots3[offset - 1, 1]))
    out[0], out[1] = product(left, right)
    for copy in halos + copies1 + copies2 + copies3:
        copy.wait_send()


def sweep(links, count_t, count_z):
    sizes = factors(count_t)
    messages = sum(sizes) - 3
    matrix = (2, 3, 3, 2, LANES)

    def space(*shape):
        return pltpu.VMEM(shape, jnp.float32)

    vmem = pl.BlockSpec(memory_space=pltpu.VMEM)
    return pl.pallas_call(
        lambda *refs: sweep_kernel(count_t, count_z, *refs),
        out_shape=[space(18, 8, LANES), space(*matrix)],
        in_specs=[pl.BlockSpec(memory_space=pl.ANY)],
        out_specs=[vmem] * 2,
        scratch_shapes=[
            space(4, 18, 2, LANES),
            space(3, 18, 2, LANES),
            space(4, 18, 2, LANES),
            space(1, 18, 1, LANES),
            space(1, 18, 1, LANES),
            space(1, 18, 1, LANES),
            space(2, 18, 1, LANES),
            space(1, 18, 1, LANES),
            space(1, 18, 1, LANES),
            space(2, 18, 1, LANES),
            space(6, 18, 8, LANES),
            space(4, 18, 8, LANES),
            space(6, 3, 18, 8, LANES),
            space(*matrix),
            space(sizes[0] - 1, *matrix),
            space(sizes[1] - 1, *matrix),
            space(sizes[2] - 1, *matrix),
            space(*matrix),
            space(*matrix),
            pltpu.SemaphoreType.DMA,
            pltpu.SemaphoreType.DMA((9,)),
            pltpu.SemaphoreType.DMA((9,)),
            pltpu.SemaphoreType.DMA((messages,)),
            pltpu.SemaphoreType.DMA((messages,)),
        ],
        compiler_params=pltpu.CompilerParams(collective_id=0, has_side_effects=True),
        name="halo_flow_loops",
    )(links)


def unpack_kernel(packed, product_in, flowed, loops):
    for i in range(18):
        for mu in range(4):
            flowed[mu, i] = packed[i, 2 * mu : 2 * mu + 2, :]
    loops[...] = product_in[...]


def unpacked(packed, loops):
    vmem = pl.BlockSpec(memory_space=pltpu.VMEM)
    return pl.pallas_call(
        unpack_kernel,
        out_shape=[
            jax.ShapeDtypeStruct((4, 18, 2, LANES), jnp.float32),
            jax.ShapeDtypeStruct(loops.shape, jnp.float32),
        ],
        in_specs=[vmem] * 2,
        out_specs=[vmem] * 2,
        name="unpack",
    )(*(pltpu.with_memory_space_constraint(v, pltpu.VMEM) for v in (packed, loops)))


def local(links):
    count_t, count_z = lax.axis_size("ta"), lax.axis_size("gz")
    packed, loops = sweep(links.reshape(4, 18, 2, LANES), count_t, count_z)
    flowed, loops = unpacked(packed, loops)
    return flowed.reshape(links.shape), loops.reshape(2, 3, 3, 1, 2, LANES)


def solution(mesh):
    return jax.shard_map(
        local,
        mesh=mesh,
        in_specs=(P(None, None, None, None, "ta", "gz", None),),
        out_specs=(
            P(None, None, None, None, "ta", "gz", None),
            P(None, None, None, "ta", "gz", None),
        ),
        check_vma=False,
    )
```

```python
import jax
import jax.numpy as jnp
from jax import lax
from jax.experimental import pallas as pl
from jax.experimental.pallas import tpu as pltpu
from jax.sharding import PartitionSpec as P

LX = 8
LY = 16
LANES = LX * LY
MESH = pl.DeviceIdType.MESH


def factors(count):
    first = 4 if count % 4 == 0 and count > 8 else 2
    rest = count // first
    third = 4 if rest % 4 == 0 and rest > 4 else 2
    return first, rest // third, third


def entry(matrix, row, col, adjoint):
    if adjoint:
        return matrix[col * 3 + row], matrix[9 + col * 3 + row], -1
    return matrix[row * 3 + col], matrix[9 + row * 3 + col], 1


def tile_product(left, right, left_adjoint=False, right_adjoint=False):
    real, imag = [], []
    for row in range(3):
        for col in range(3):
            re = im = None
            for mid in range(3):
                a, b, s = entry(left, row, mid, left_adjoint)
                c, d, r = entry(right, mid, col, right_adjoint)
                ac, bd, ad, bc = a * c, b * d, a * d, b * c
                re_term = ac - bd if s * r > 0 else ac + bd
                re = re_term if re is None else re + re_term
                if im is None:
                    if r > 0:
                        im = ad + bc if s > 0 else ad - bc
                    else:
                        im = bc - ad if s > 0 else -(ad + bc)
                else:
                    im = im + ad if r > 0 else im - ad
                    im = im + bc if s > 0 else im - bc
            real.append(re)
            imag.append(im)
    return real + imag


def tile_helpers():
    group = lax.broadcasted_iota(jnp.int32, (8, LANES), 0) // 2
    y = lax.broadcasted_iota(jnp.int32, (8, LANES), 1) % LY

    def pick(tiles):
        rest = jnp.where(group == 2, tiles[2], tiles[3])
        return jnp.where(group == 0, tiles[0], jnp.where(group == 1, tiles[1], rest))

    def x_plus(tile):
        return pltpu.roll(tile, LANES - LY, 1)

    def x_minus(tile):
        return pltpu.roll(tile, LY, 1)

    def y_plus(tile):
        return jnp.where(
            y == LY - 1, pltpu.roll(tile, LY - 1, 1), pltpu.roll(tile, LANES - 1, 1)
        )

    def y_minus(tile):
        return jnp.where(
            y == 0, pltpu.roll(tile, LANES - LY + 1, 1), pltpu.roll(tile, 1, 1)
        )

    return group, pick, x_plus, x_minus, y_plus, y_minus


def plus_unity(matrix):
    return [v + 1.0 if i in (0, 4, 8) else v for i, v in enumerate(matrix)]


def flowed_link(link, total):
    omega = tile_product(link, total)
    trace = (omega[9] + omega[13] + omega[17]) * (1.0 / 3.0)
    generator = [None] * 18
    for row in range(3):
        for col in range(3):
            a, b = row * 3 + col, col * 3 + row
            generator[a] = -0.125 * (omega[a] - omega[b])
            part = 0.5 * (omega[9 + a] + omega[9 + b])
            if row == col:
                part = part - trace
            generator[9 + a] = -0.25 * part
    series = plus_unity([v * (1.0 / 6.0) for v in generator])
    for order in range(5, 0, -1):
        series = tile_product(generator, series)
        series = plus_unity([v * (1.0 / order) for v in series])
    return tile_product(series, link)


def both_staples(a, b, c, d, e, f):
    upper = tile_product(tile_product(a, b, False, True), c, False, True)
    lower = tile_product(tile_product(d, e, True, True), f)
    return [v + w for v, w in zip(upper, lower)]


def pack_own(u, pk):
    for i in range(18):
        for mu in range(4):
            pk[0, i, 2 * mu : 2 * mu + 2, :] = u[mu, i]


KEPT = tuple(range(6)) + tuple(range(9, 15))


def restore_row(tiles):
    for col in range(3):
        k, m = (col + 1) % 3, (col + 2) % 3
        ak, am, bk, bm = tiles[k], tiles[m], tiles[3 + k], tiles[3 + m]
        ck, cm, dk, dm = tiles[9 + k], tiles[9 + m], tiles[12 + k], tiles[12 + m]
        tiles[6 + col] = (ak * bm - ck * dm) - (am * bk - cm * dk)
        tiles[15 + col] = (am * dk + cm * bk) - (ak * dm + ck * bm)


def flow_line(u, tp, cz, zm0, zm3, zp0, pk, sides, line):
    group, pick, x_plus, x_minus, y_plus, y_minus = tile_helpers()
    for i in KEPT:
        for mu in range(1, 4):
            pk[1, i, 2 * mu : 2 * mu + 2, :] = tp[mu - 1, i]
        sides[0, i, 6:7, :] = u[0, i, 1:2]
        sides[0, i, 7:8, :] = zp0[0, i]
        sides[1, i, 6:7, :] = cz[0, i]
        sides[1, i, 7:8, :] = tp[2, i, 0:1]
        sides[2, i, 6:7, :] = zm0[0, i]
        sides[2, i, 7:8, :] = u[0, i, 0:1]
        sides[3, i, 6:7, :] = zm3[0, i]
        sides[3, i, 7:8, :] = u[3, i, 0:1]
    restore_row(pk.at[1])
    for f in range(4):
        restore_row(sides.at[f])
    first = group == 0

    def spread(tile):
        tile = tile + pltpu.roll(tile, 4, 0)
        return tile + pltpu.roll(tile, 2, 0)

    here = [pk[0, i] for i in range(18)]
    ahead = [pk[1, i] for i in range(18)]
    link = [spread(jnp.where(first, tile, 0.0)) for tile in here]
    side = [[sides[f, i] for i in range(18)] for f in range(4)]
    b = [pick([v, x_plus(v), y_plus(v), s]) for v, s in zip(link, side[0])]
    d = [pick([v, x_minus(v), y_minus(v), s]) for v, s in zip(ahead, side[1])]
    e = [pick([v, x_minus(v), y_minus(v), s]) for v, s in zip(link, side[2])]
    f = [pick([v, x_minus(v), y_minus(v), s]) for v, s in zip(here, side[3])]
    total = both_staples(ahead, b, here, d, e, f)
    total = [spread(jnp.where(first, 0.0, v)) for v in total]
    result = flowed_link(link, total)
    for i in range(18):
        line[i // 9, (i // 3) % 3, i % 3] = result[i][0:2]


def flow_all(u, tm, ct, zm12, zp12, pk, sides, fields, result):
    group, pick, x_plus, x_minus, y_plus, y_minus = tile_helpers()
    for i in range(18):
        below = (sides[2, i, 6:7], zm12[0, i], zm12[1, i], sides[3, i, 6:7])
        above = (sides[0, i, 7:8], zp12[0, i], zp12[1, i])
        for mu in range(4):
            pk[2, i, 2 * mu : 2 * mu + 2, :] = tm[mu, i]
            pk[4, i, 2 * mu : 2 * mu + 1, :] = below[mu]
            pk[4, i, 2 * mu + 1 : 2 * mu + 2, :] = u[mu, i, 0:1]
            if mu < 3:
                pk[3, i, 2 * mu : 2 * mu + 1, :] = u[mu, i, 1:2]
                pk[3, i, 2 * mu + 1 : 2 * mu + 2, :] = above[mu]
        pk[5, i, 0:1, :] = tm[0, i, 1:2]
        pk[5, i, 1:2, :] = ct[0, i]
        pk[5, i, 6:8, :] = sides[1, i, 6:8]

    def lowered(tile, k):
        return pltpu.roll(tile, 8 - 2 * k, 0)

    def pack_fields(i):
        here, t_up, t_down, z_up, z_down, corner = (pk[f, i] for f in range(6))
        up = [t_up, x_plus(here), y_plus(here), z_up]
        down = [t_down, x_minus(here), y_minus(here), z_down]
        base = pick(down)
        t_side = [None, corner, y_plus(t_down), x_plus(t_down)]
        z_side = [None, y_plus(z_down), x_plus(z_down), corner]
        for k in range(1, 4):
            ahead = pick([up[(nu - k) % 4] for nu in range(4)])
            behind = pick([down[(nu - k) % 4] for nu in range(4)])
            cross = pick([t_side[k], x_minus(ahead), y_minus(ahead), z_side[k]])
            fields[0, k - 1, i] = lowered(ahead, k)
            fields[1, 3 - k, i] = ahead
            fields[2, k - 1, i] = lowered(here, k)
            fields[3, k - 1, i] = lowered(cross, k)
            fields[4, 3 - k, i] = behind
            fields[5, k - 1, i] = lowered(base, k)

    for i in range(18):
        pack_fields(i)
    total = None
    for k in range(3):
        mats = [[fields[field, k, i] for i in range(18)] for field in range(6)]
        both = both_staples(*mats)
        total = both if total is None else [a + b for a, b in zip(total, both)]
    flowed = flowed_link([pk[0, i] for i in range(18)], total)
    for i in range(18):
        result[i] = flowed[i]


def product(left, right):
    re = im = None
    for mid in range(3):
        a, b = left[0][:, mid : mid + 1], left[1][:, mid : mid + 1]
        c, d = right[0][mid : mid + 1], right[1][mid : mid + 1]
        re_term, im_term = a * c - b * d, a * d + b * c
        re = re_term if re is None else re + re_term
        im = im_term if im is None else im + im_term
    return re, im


def sweep_kernel(count_t, count_z, links, result, out, u, tp, tm, cz, ct, zm0, zm12, zm3, zp0, zp12,
                 pk, sides, fields, line, slots1, slots2, slots3, row_total, plane_total,
                 own_sem, halo_send, halo_recv, send, recv):
    t = lax.axis_index("ta")
    z = lax.axis_index("gz")
    t_next, t_prev = lax.rem(t + 1, count_t), lax.rem(t + count_t - 1, count_t)
    z_next, z_prev = lax.rem(z + 1, count_z), lax.rem(z + count_z - 1, count_z)
    sizes = factors(count_t)
    strides = (1, sizes[0], sizes[0] * sizes[1])
    digits = [lax.rem(t // stride, size) for stride, size in zip(strides, sizes)]
    slots = (slots1, slots2, slots3)

    def peer(stage, offset):
        size, stride, digit = sizes[stage], strides[stage], digits[stage]
        moved = lax.rem(digit + size - offset, size)
        return (t + (moved - digit) * stride, z)

    halo_peers = [
        (t_prev, z), (t_next, z), (t, z_next), (t, z_prev), (t_prev, z_next), (t_next, z_prev)
    ]
    peers = halo_peers + [peer(s, d) for s in range(3) for d in range(1, sizes[s])]
    barrier = pltpu.get_barrier_semaphore()
    for other in peers:
        pl.semaphore_signal(barrier, inc=1, device_id=other, device_id_type=MESH)
    own = pltpu.make_async_copy(links, u, own_sem)
    own.start()
    pl.semaphore_wait(barrier, len(peers))

    def two_rows(source, target, other):
        return [
            (source.at[:, pl.ds(first, 6)], target.at[:, pl.ds(first, 6)], other)
            for first in (0, 9)
        ]

    def layer(first, size, row):
        return links.at[pl.ds(first, size), :, pl.ds(row, 1), :]

    critical = [
        (layer(3, 1, 1), cz, (t_prev, z_next)),
        (layer(0, 1, 1), zm0, (t, z_next)),
        (layer(3, 1, 1), zm3, (t, z_next)),
        (layer(0, 1, 0), zp0, (t, z_prev)),
        (links.at[pl.ds(1, 3)], tp, (t_prev, z)),
    ]
    plan = [item for whole in critical for item in two_rows(*whole)] + [
        (layer(0, 1, 0), ct, (t_next, z_prev)),
        (links, tm, (t_next, z)),
        (layer(1, 2, 1), zm12, (t, z_next)),
        (layer(1, 2, 0), zp12, (t, z_prev)),
    ]
    halos = [
        pltpu.make_async_remote_copy(
            src_ref=source,
            dst_ref=target,
            send_sem=halo_send.at[index],
            recv_sem=halo_recv.at[index],
            device_id=other,
            device_id_type=MESH,
        )
        for index, (source, target, other) in enumerate(plan)
    ]
    for copy in halos[:12]:
        copy.start()
    own.wait()
    pack_own(u, pk)
    for copy in halos[:10]:
        copy.wait_recv()
    for copy in halos[12:]:
        copy.start()
    flow_line(u, tp, cz, zm0, zm3, zp0, pk, sides, line)

    shape = (3, 3) + line.shape[-2:]
    diagonal = [
        [jnp.full(shape[2:], 1.0 if a == b else 0.0, jnp.float32) for b in range(3)]
        for a in range(3)
    ]
    unity = jnp.stack([jnp.stack(row) for row in diagonal])
    nought = jnp.zeros(shape, jnp.float32)
    start = [0, sizes[0] - 1, sizes[0] + sizes[1] - 2]

    def share(stage, source):
        copies = []
        for offset in range(1, sizes[stage]):
            index = start[stage] + offset - 1
            copies.append(
                pltpu.make_async_remote_copy(
                    src_ref=source,
                    dst_ref=slots[stage].at[offset - 1],
                    send_sem=send.at[index],
                    recv_sem=recv.at[index],
                    device_id=peer(stage, offset),
                    device_id_type=MESH,
                )
            )
        size = sizes[stage]
        for offset in sorted(range(1, size), key=lambda d: -min(d, size - d)):
            copies[offset - 1].start()
        return copies

    def ordered(stage, copies):
        after = before = None
        for offset in range(1, sizes[stage]):
            copies[offset - 1].wait_recv()
            re, im = slots[stage][offset - 1, 0], slots[stage][offset - 1, 1]
            inside = digits[stage] + offset < sizes[stage]
            high = (jnp.where(inside, re, unity), jnp.where(inside, im, nought))
            low = (jnp.where(inside, unity, re), jnp.where(inside, nought, im))
            after = high if after is None else product(after, high)
            before = low if before is None else product(before, low)
        return after, before

    copies1 = share(0, line)
    row_after, row_before = ordered(0, copies1)
    row_after = product((line[0], line[1]), row_after)
    row = product(row_before, row_after)
    row_total[0], row_total[1] = row
    copies2 = share(1, row_total)
    plane_after, plane_before = ordered(1, copies2)
    plane = product(plane_before, product(row, plane_after))
    plane_total[0], plane_total[1] = plane
    copies3 = share(2, plane_total)
    left = product(row_after, plane_after)
    right = product(plane_before, row_before)
    for copy in halos[10:]:
        copy.wait_recv()
    flow_all(u, tm, ct, zm12, zp12, pk, sides, fields, result)
    for offset in range(1, sizes[2]):
        copies3[offset - 1].wait_recv()
        left = product(left, (slots3[offset - 1, 0], slots3[offset - 1, 1]))
    out[0], out[1] = product(left, right)
    for copy in halos + copies1 + copies2 + copies3:
        copy.wait_send()


def sweep(links, count_t, count_z):
    sizes = factors(count_t)
    messages = sum(sizes) - 3
    matrix = (2, 3, 3, 2, LANES)

    def space(*shape):
        return pltpu.VMEM(shape, jnp.float32)

    vmem = pl.BlockSpec(memory_space=pltpu.VMEM)
    return pl.pallas_call(
        lambda *refs: sweep_kernel(count_t, count_z, *refs),
        out_shape=[space(18, 8, LANES), space(*matrix)],
        in_specs=[pl.BlockSpec(memory_space=pl.ANY)],
        out_specs=[vmem] * 2,
        scratch_shapes=[
            space(4, 18, 2, LANES),
            space(3, 18, 2, LANES),
            space(4, 18, 2, LANES),
            space(1, 18, 1, LANES),
            space(1, 18, 1, LANES),
            space(1, 18, 1, LANES),
            space(2, 18, 1, LANES),
            space(1, 18, 1, LANES),
            space(1, 18, 1, LANES),
            space(2, 18, 1, LANES),
            space(6, 18, 8, LANES),
            space(4, 18, 8, LANES),
            space(6, 3, 18, 8, LANES),
            space(*matrix),
            space(sizes[0] - 1, *matrix),
            space(sizes[1] - 1, *matrix),
            space(sizes[2] - 1, *matrix),
            space(*matrix),
            space(*matrix),
            pltpu.SemaphoreType.DMA,
            pltpu.SemaphoreType.DMA((14,)),
            pltpu.SemaphoreType.DMA((14,)),
            pltpu.SemaphoreType.DMA((messages,)),
            pltpu.SemaphoreType.DMA((messages,)),
        ],
        compiler_params=pltpu.CompilerParams(collective_id=0, has_side_effects=True),
        name="halo_flow_loops",
    )(links)


def unpack_kernel(packed, product_in, flowed, loops):
    for i in range(18):
        for mu in range(4):
            flowed[mu, i] = packed[i, 2 * mu : 2 * mu + 2, :]
    loops[...] = product_in[...]


def unpacked(packed, loops):
    vmem = pl.BlockSpec(memory_space=pltpu.VMEM)
    return pl.pallas_call(
        unpack_kernel,
        out_shape=[
            jax.ShapeDtypeStruct((4, 18, 2, LANES), jnp.float32),
            jax.ShapeDtypeStruct(loops.shape, jnp.float32),
        ],
        in_specs=[vmem] * 2,
        out_specs=[vmem] * 2,
        name="unpack",
    )(*(pltpu.with_memory_space_constraint(v, pltpu.VMEM) for v in (packed, loops)))


def local(links):
    count_t, count_z = lax.axis_size("ta"), lax.axis_size("gz")
    packed, loops = sweep(links.reshape(4, 18, 2, LANES), count_t, count_z)
    flowed, loops = unpacked(packed, loops)
    return flowed.reshape(links.shape), loops.reshape(2, 3, 3, 1, 2, LANES)


def solution(mesh):
    return jax.shard_map(
        local,
        mesh=mesh,
        in_specs=(P(None, None, None, None, "ta", "gz", None),),
        out_specs=(
            P(None, None, None, None, "ta", "gz", None),
            P(None, None, None, "ta", "gz", None),
        ),
        check_vma=False,
    )
```

```python
import jax
import jax.numpy as jnp
from jax import lax
from jax.experimental import pallas as pl
from jax.experimental.pallas import tpu as pltpu
from jax.sharding import PartitionSpec as P

LX = 8
LY = 16
LANES = LX * LY
MESH = pl.DeviceIdType.MESH


def factors(count):
    first = 4 if count % 4 == 0 and count > 8 else 2
    rest = count // first
    third = 4 if rest % 4 == 0 and rest > 4 else 2
    return first, rest // third, third


def entry(matrix, row, col, adjoint):
    if adjoint:
        return matrix[col * 3 + row], matrix[9 + col * 3 + row], -1
    return matrix[row * 3 + col], matrix[9 + row * 3 + col], 1


def tile_product(left, right, left_adjoint=False, right_adjoint=False):
    real, imag = [], []
    for row in range(3):
        for col in range(3):
            re = im = None
            for mid in range(3):
                a, b, s = entry(left, row, mid, left_adjoint)
                c, d, r = entry(right, mid, col, right_adjoint)
                ac, bd, ad, bc = a * c, b * d, a * d, b * c
                re_term = ac - bd if s * r > 0 else ac + bd
                re = re_term if re is None else re + re_term
                if im is None:
                    if r > 0:
                        im = ad + bc if s > 0 else ad - bc
                    else:
                        im = bc - ad if s > 0 else -(ad + bc)
                else:
                    im = im + ad if r > 0 else im - ad
                    im = im + bc if s > 0 else im - bc
            real.append(re)
            imag.append(im)
    return real + imag


def tile_helpers():
    group = lax.broadcasted_iota(jnp.int32, (8, LANES), 0) // 2
    y = lax.broadcasted_iota(jnp.int32, (8, LANES), 1) % LY

    def pick(tiles):
        rest = jnp.where(group == 2, tiles[2], tiles[3])
        return jnp.where(group == 0, tiles[0], jnp.where(group == 1, tiles[1], rest))

    def x_plus(tile):
        return pltpu.roll(tile, LANES - LY, 1)

    def x_minus(tile):
        return pltpu.roll(tile, LY, 1)

    def y_plus(tile):
        return jnp.where(
            y == LY - 1, pltpu.roll(tile, LY - 1, 1), pltpu.roll(tile, LANES - 1, 1)
        )

    def y_minus(tile):
        return jnp.where(
            y == 0, pltpu.roll(tile, LANES - LY + 1, 1), pltpu.roll(tile, 1, 1)
        )

    return group, pick, x_plus, x_minus, y_plus, y_minus


def plus_unity(matrix):
    return [v + 1.0 if i in (0, 4, 8) else v for i, v in enumerate(matrix)]


def flowed_link(link, total):
    omega = tile_product(link, total)
    trace = (omega[9] + omega[13] + omega[17]) * (1.0 / 3.0)
    generator = [None] * 18
    for row in range(3):
        for col in range(3):
            a, b = row * 3 + col, col * 3 + row
            generator[a] = -0.125 * (omega[a] - omega[b])
            part = 0.5 * (omega[9 + a] + omega[9 + b])
            if row == col:
                part = part - trace
            generator[9 + a] = -0.25 * part
    series = plus_unity([v * (1.0 / 6.0) for v in generator])
    for order in range(5, 0, -1):
        series = tile_product(generator, series)
        series = plus_unity([v * (1.0 / order) for v in series])
    return tile_product(series, link)


def both_staples(a, b, c, d, e, f):
    upper = tile_product(tile_product(a, b, False, True), c, False, True)
    lower = tile_product(tile_product(d, e, True, True), f)
    return [v + w for v, w in zip(upper, lower)]


def pack_own(u, pk):
    for i in range(18):
        for mu in range(4):
            pk[0, i, 2 * mu : 2 * mu + 2, :] = u[mu, i]


def flow_line(u, tp, cz, zm0, zm3, zp0, pk, sides, line):
    group, pick, x_plus, x_minus, y_plus, y_minus = tile_helpers()
    for i in range(18):
        for mu in range(1, 4):
            pk[1, i, 2 * mu : 2 * mu + 2, :] = tp[mu - 1, i]
        sides[0, i, 6:7, :] = u[0, i, 1:2]
        sides[0, i, 7:8, :] = zp0[0, i]
        sides[1, i, 6:7, :] = cz[0, i]
        sides[1, i, 7:8, :] = tp[2, i, 0:1]
        sides[2, i, 6:7, :] = zm0[0, i]
        sides[2, i, 7:8, :] = u[0, i, 0:1]
        sides[3, i, 6:7, :] = zm3[0, i]
        sides[3, i, 7:8, :] = u[3, i, 0:1]
    first = group == 0

    def spread(tile):
        tile = tile + pltpu.roll(tile, 4, 0)
        return tile + pltpu.roll(tile, 2, 0)

    here = [pk[0, i] for i in range(18)]
    ahead = [pk[1, i] for i in range(18)]
    link = [spread(jnp.where(first, tile, 0.0)) for tile in here]
    side = [[sides[f, i] for i in range(18)] for f in range(4)]
    b = [pick([v, x_plus(v), y_plus(v), s]) for v, s in zip(link, side[0])]
    d = [pick([v, x_minus(v), y_minus(v), s]) for v, s in zip(ahead, side[1])]
    e = [pick([v, x_minus(v), y_minus(v), s]) for v, s in zip(link, side[2])]
    f = [pick([v, x_minus(v), y_minus(v), s]) for v, s in zip(here, side[3])]
    total = both_staples(ahead, b, here, d, e, f)
    total = [spread(jnp.where(first, 0.0, v)) for v in total]
    result = flowed_link(link, total)
    for i in range(18):
        line[i // 9, (i // 3) % 3, i % 3] = result[i][0:2]


def flow_all(u, tp, tm, cz, ct, zm0, zm12, zm3, zp0, zp12, pk, fields, result):
    group, pick, x_plus, x_minus, y_plus, y_minus = tile_helpers()
    for i in range(18):
        below = (zm0[0, i], zm12[0, i], zm12[1, i], zm3[0, i])
        above = (zp0[0, i], zp12[0, i], zp12[1, i])
        for mu in range(4):
            pk[2, i, 2 * mu : 2 * mu + 2, :] = tm[mu, i]
            pk[4, i, 2 * mu : 2 * mu + 1, :] = below[mu]
            pk[4, i, 2 * mu + 1 : 2 * mu + 2, :] = u[mu, i, 0:1]
            if mu < 3:
                pk[3, i, 2 * mu : 2 * mu + 1, :] = u[mu, i, 1:2]
                pk[3, i, 2 * mu + 1 : 2 * mu + 2, :] = above[mu]
        pk[5, i, 0:1, :] = tm[0, i, 1:2]
        pk[5, i, 1:2, :] = ct[0, i]
        pk[5, i, 6:7, :] = cz[0, i]
        pk[5, i, 7:8, :] = tp[2, i, 0:1]

    def lowered(tile, k):
        return pltpu.roll(tile, 8 - 2 * k, 0)

    def pack_fields(i):
        here, t_up, t_down, z_up, z_down, corner = (pk[f, i] for f in range(6))
        up = [t_up, x_plus(here), y_plus(here), z_up]
        down = [t_down, x_minus(here), y_minus(here), z_down]
        base = pick(down)
        t_side = [None, corner, y_plus(t_down), x_plus(t_down)]
        z_side = [None, y_plus(z_down), x_plus(z_down), corner]
        for k in range(1, 4):
            ahead = pick([up[(nu - k) % 4] for nu in range(4)])
            behind = pick([down[(nu - k) % 4] for nu in range(4)])
            cross = pick([t_side[k], x_minus(ahead), y_minus(ahead), z_side[k]])
            fields[0, k - 1, i] = lowered(ahead, k)
            fields[1, 3 - k, i] = ahead
            fields[2, k - 1, i] = lowered(here, k)
            fields[3, k - 1, i] = lowered(cross, k)
            fields[4, 3 - k, i] = behind
            fields[5, k - 1, i] = lowered(base, k)

    for i in range(18):
        pack_fields(i)
    total = None
    for k in range(3):
        mats = [[fields[field, k, i] for i in range(18)] for field in range(6)]
        both = both_staples(*mats)
        total = both if total is None else [a + b for a, b in zip(total, both)]
    flowed = flowed_link([pk[0, i] for i in range(18)], total)
    for i in range(18):
        result[i] = flowed[i]


def product(left, right):
    re = im = None
    for mid in range(3):
        a, b = left[0][:, mid : mid + 1], left[1][:, mid : mid + 1]
        c, d = right[0][mid : mid + 1], right[1][mid : mid + 1]
        re_term, im_term = a * c - b * d, a * d + b * c
        re = re_term if re is None else re + re_term
        im = im_term if im is None else im + im_term
    return re, im


def sweep_kernel(count_t, count_z, links, result, out, u, tp, tm, cz, ct, zm0, zm12, zm3, zp0, zp12,
                 pk, sides, fields, line, slots1, slots2, slots3, row_total, plane_total,
                 own_sem, halo_send, halo_recv, send, recv):
    t = lax.axis_index("ta")
    z = lax.axis_index("gz")
    t_next, t_prev = lax.rem(t + 1, count_t), lax.rem(t + count_t - 1, count_t)
    z_next, z_prev = lax.rem(z + 1, count_z), lax.rem(z + count_z - 1, count_z)
    sizes = factors(count_t)
    strides = (1, sizes[0], sizes[0] * sizes[1])
    digits = [lax.rem(t // stride, size) for stride, size in zip(strides, sizes)]
    slots = (slots1, slots2, slots3)

    def peer(stage, offset):
        size, stride, digit = sizes[stage], strides[stage], digits[stage]
        moved = lax.rem(digit + size - offset, size)
        return (t + (moved - digit) * stride, z)

    halo_peers = [
        (t_prev, z), (t_next, z), (t, z_next), (t, z_prev), (t_prev, z_next), (t_next, z_prev)
    ]
    peers = halo_peers + [peer(s, d) for s in range(3) for d in range(1, sizes[s])]
    barrier = pltpu.get_barrier_semaphore()
    for other in peers:
        pl.semaphore_signal(barrier, inc=1, device_id=other, device_id_type=MESH)
    own = pltpu.make_async_copy(links, u, own_sem)
    own.start()
    pl.semaphore_wait(barrier, len(peers))

    def layer(first, size, row):
        return links.at[pl.ds(first, size), :, pl.ds(row, 1), :]

    plan = [
        (layer(3, 1, 1), cz, (t_prev, z_next)),
        (layer(0, 1, 1), zm0, (t, z_next)),
        (layer(3, 1, 1), zm3, (t, z_next)),
        (layer(0, 1, 0), zp0, (t, z_prev)),
        (links.at[pl.ds(1, 3)], tp, (t_prev, z)),
        (layer(0, 1, 0), ct, (t_next, z_prev)),
        (links, tm, (t_next, z)),
        (layer(1, 2, 1), zm12, (t, z_next)),
        (layer(1, 2, 0), zp12, (t, z_prev)),
    ]
    halos = [
        pltpu.make_async_remote_copy(
            src_ref=source,
            dst_ref=target,
            send_sem=halo_send.at[index],
            recv_sem=halo_recv.at[index],
            device_id=other,
            device_id_type=MESH,
        )
        for index, (source, target, other) in enumerate(plan)
    ]
    for copy in halos[:7]:
        copy.start()
    own.wait()
    pack_own(u, pk)
    for copy in halos[:5]:
        copy.wait_recv()
    for copy in halos[7:]:
        copy.start()
    flow_line(u, tp, cz, zm0, zm3, zp0, pk, sides, line)

    diagonal = [
        [jnp.full((4, LANES), 1.0 if a == b else 0.0, jnp.float32) for b in range(3)]
        for a in range(3)
    ]
    unity_rows = jnp.stack([jnp.stack(row) for row in diagonal])
    start = [0, sizes[0] - 1, sizes[0] + sizes[1] - 2]

    def share(stage, source):
        copies = []
        for offset in range(1, sizes[stage]):
            index = start[stage] + offset - 1
            copies.append(
                pltpu.make_async_remote_copy(
                    src_ref=source,
                    dst_ref=slots[stage].at[offset - 1],
                    send_sem=send.at[index],
                    recv_sem=recv.at[index],
                    device_id=peer(stage, offset),
                    device_id_type=MESH,
                )
            )
        size = sizes[stage]
        for offset in sorted(range(1, size), key=lambda d: -min(d, size - d)):
            copies[offset - 1].start()
        return copies

    def ordered(stage, copies):
        both = None
        rows = lax.broadcasted_iota(jnp.int32, (3, 3, 4, LANES), 2)
        for offset in range(1, sizes[stage]):
            copies[offset - 1].wait_recv()
            inside = (digits[stage] + offset < sizes[stage]).astype(jnp.int32)
            used = (rows // 2) + inside == 1
            parts = [slots[stage][offset - 1, c] for c in range(2)]
            re, im = (jnp.concatenate([part, part], axis=2) for part in parts)
            factor = (jnp.where(used, re, unity_rows), jnp.where(used, im, 0.0))
            both = factor if both is None else product(both, factor)
        after = tuple(part[:, :, 0:2] for part in both)
        before = tuple(part[:, :, 2:4] for part in both)
        return after, before

    copies1 = share(0, line)
    row_after, row_before = ordered(0, copies1)
    row_after = product((line[0], line[1]), row_after)
    row = product(row_before, row_after)
    row_total[0], row_total[1] = row
    copies2 = share(1, row_total)
    plane_after, plane_before = ordered(1, copies2)
    plane = product(plane_before, product(row, plane_after))
    plane_total[0], plane_total[1] = plane
    copies3 = share(2, plane_total)
    left = product(row_after, plane_after)
    right = product(plane_before, row_before)
    for copy in halos[5:]:
        copy.wait_recv()
    flow_all(u, tp, tm, cz, ct, zm0, zm12, zm3, zp0, zp12, pk, fields, result)
    for offset in range(1, sizes[2]):
        copies3[offset - 1].wait_recv()
        left = product(left, (slots3[offset - 1, 0], slots3[offset - 1, 1]))
    out[0], out[1] = product(left, right)
    for copy in halos + copies1 + copies2 + copies3:
        copy.wait_send()


def sweep(links, count_t, count_z):
    sizes = factors(count_t)
    messages = sum(sizes) - 3
    matrix = (2, 3, 3, 2, LANES)

    def space(*shape):
        return pltpu.VMEM(shape, jnp.float32)

    vmem = pl.BlockSpec(memory_space=pltpu.VMEM)
    return pl.pallas_call(
        lambda *refs: sweep_kernel(count_t, count_z, *refs),
        out_shape=[space(18, 8, LANES), space(*matrix)],
        in_specs=[pl.BlockSpec(memory_space=pl.ANY)],
        out_specs=[vmem] * 2,
        scratch_shapes=[
            space(4, 18, 2, LANES),
            space(3, 18, 2, LANES),
            space(4, 18, 2, LANES),
            space(1, 18, 1, LANES),
            space(1, 18, 1, LANES),
            space(1, 18, 1, LANES),
            space(2, 18, 1, LANES),
            space(1, 18, 1, LANES),
            space(1, 18, 1, LANES),
            space(2, 18, 1, LANES),
            space(6, 18, 8, LANES),
            space(4, 18, 8, LANES),
            space(6, 3, 18, 8, LANES),
            space(*matrix),
            space(sizes[0] - 1, *matrix),
            space(sizes[1] - 1, *matrix),
            space(sizes[2] - 1, *matrix),
            space(*matrix),
            space(*matrix),
            pltpu.SemaphoreType.DMA,
            pltpu.SemaphoreType.DMA((9,)),
            pltpu.SemaphoreType.DMA((9,)),
            pltpu.SemaphoreType.DMA((messages,)),
            pltpu.SemaphoreType.DMA((messages,)),
        ],
        compiler_params=pltpu.CompilerParams(collective_id=0, has_side_effects=True),
        name="halo_flow_loops",
    )(links)


def unpack_kernel(packed, product_in, flowed, loops):
    for i in range(18):
        for mu in range(4):
            flowed[mu, i] = packed[i, 2 * mu : 2 * mu + 2, :]
    loops[...] = product_in[...]


def unpacked(packed, loops):
    vmem = pl.BlockSpec(memory_space=pltpu.VMEM)
    return pl.pallas_call(
        unpack_kernel,
        out_shape=[
            jax.ShapeDtypeStruct((4, 18, 2, LANES), jnp.float32),
            jax.ShapeDtypeStruct(loops.shape, jnp.float32),
        ],
        in_specs=[vmem] * 2,
        out_specs=[vmem] * 2,
        name="unpack",
    )(*(pltpu.with_memory_space_constraint(v, pltpu.VMEM) for v in (packed, loops)))


def local(links):
    count_t, count_z = lax.axis_size("ta"), lax.axis_size("gz")
    packed, loops = sweep(links.reshape(4, 18, 2, LANES), count_t, count_z)
    flowed, loops = unpacked(packed, loops)
    return flowed.reshape(links.shape), loops.reshape(2, 3, 3, 1, 2, LANES)


def solution(mesh):
    return jax.shard_map(
        local,
        mesh=mesh,
        in_specs=(P(None, None, None, None, "ta", "gz", None),),
        out_specs=(
            P(None, None, None, None, "ta", "gz", None),
            P(None, None, None, "ta", "gz", None),
        ),
        check_vma=False,
    )
```
